128 devices in a mesh: atm: 16 (over z, x), ocn: 8 (over y, core).
Axes of the slice: x: 4, y: 4, z: 4, core: 2. Of those that a mesh axis runs over, the one named last changes fastest.
Arguments:
- atm_state: float32 [3, 63, 262144], P(None, None, ('atm', 'ocn')), may hold values from -6 to 6
- diffusivity: float32 [62, 262144], P(None, ('atm', 'ocn')), may hold values from 0.1 to 10
- send_slot: int32 [128, 256], P(('atm', 'ocn')), may hold values from 0 to 511, as said below
- atm_block: int32 [128, 256], P(('atm', 'ocn')), may hold values from 0 to 15
- recv_row: int32 [128, 512], P(('atm', 'ocn')), may hold values from -1 to 31, as said below
- remap_weight: bfloat16 [32768, 128, 128], P(('atm', 'ocn')), may hold values from 0 to 0.001953125
- ocean_tracer: float32 [3, 75, 512, 1024], P(None, None, 'atm', 'ocn'), may hold values from -6 to 6
- ocean_velocity: float32 [2, 75, 512, 1024], P(None, None, 'atm', 'ocn'), may hold values from -0.24 to 0.24
- exchange_coef: float32 [512, 1024], P('atm', 'ocn'), may hold values from 0.2 to 5
- surface_kind: int32 [512, 1024], P('atm', 'ocn'), may hold values from 0 to 2
- ice_surface: float32 [3, 512, 1024], P(None, 'atm', 'ocn'), may hold values from -6 to 6
Outputs:
- atm_new: float32 [3, 63, 262144], P(None, None, ('atm', 'ocn'))
- ocean_new: float32 [3, 75, 512, 1024], P(None, None, 'atm', 'ocn')
The draws below stay inside these ranges and needn't reach their ends.
Inputs may be any that keep to these rules, and one draw needn't show every extreme that they name: `send_slot`: entry [s, b] = d * 4 + k names owner d and slot k for block b of device s; entries of a row are distinct. Each device sends 4 blocks to itself, and one owner receives 4 blocks from every device. `recv_row`: entry [d, s * 4 + k] is the row of owner d's tile that receives the block that device s sends to slot k of d, and -1 exactly where device s sends nothing to that slot.
All inputs are finite; a program needn't handle non-finite values.
Results may differ from the reference program's by a relative error of at most 0.0003.
Values may be sent and summed in bfloat16 or wider, within the bound.
A program may use at most 192 MiB of HBM per device.

```python
import math
import jax
import jax.numpy as jnp
from jax import lax

NV = 3
LEV = 63
OLEV = 75
ORX = 128
CAP = 4
NSUB = 4
ORY = 32
NBLK = 256
ABLK = 16
COLUMNS = 262144
NY_O = 512
NX_O = 1024
N_OCN = 8
DEVICES = 128


def routing_table(key):
    base = jax.random.fold_in(key, 9173)
    key_hot, key_score, key_rows = jax.random.split(base, 3)
    slot_count = DEVICES * CAP
    slot_ids = jnp.arange(slot_count, dtype=jnp.int32)
    owners = slot_ids // CAP
    sources = jnp.arange(DEVICES, dtype=jnp.int32)[:, None]
    hottest = jax.random.randint(key_hot, (), 0, DEVICES, dtype=jnp.int32)
    noise_bits = jax.random.randint(key_score, (DEVICES, slot_count), 0, 2 ** 29 // slot_count, dtype=jnp.int32)
    scores = noise_bits * slot_count + slot_ids[None, :]
    scores = jnp.where(owners[None, :] == hottest, 2 ** 29 + slot_ids[None, :], scores)
    scores = jnp.where(owners[None, :] == sources, 2 ** 30 + slot_ids[None, :], scores)
    top_values, top_index = lax.top_k(scores, NBLK)
    occupied = scores >= top_values[:, -1:]
    rows_drawn = jax.random.randint(key_rows, (DEVICES, DEVICES, CAP), 0, ORY, dtype=jnp.int32)
    balanced = (jnp.arange(DEVICES, dtype=jnp.int32)[:, None] * CAP + jnp.arange(CAP, dtype=jnp.int32)[None, :]) % ORY
    is_hot = jnp.arange(DEVICES, dtype=jnp.int32)[:, None, None] == hottest
    rows_drawn = jnp.where(is_hot, balanced[None], rows_drawn)
    is_live = occupied.reshape(DEVICES, DEVICES, CAP).transpose(1, 0, 2)
    received = jnp.where(is_live, rows_drawn, -1).reshape(DEVICES, slot_count)
    return (top_index.astype(jnp.int32), received.astype(jnp.int32))


def draw_send_slot(key, part):
    return routing_table(key)[0]


def draw_recv_row(key, part):
    return routing_table(key)[1]


def set_ends(drawn, key, low, largest):
    dims = drawn.shape
    index_at = [jax.random.randint(jax.random.fold_in(key, axis), (), 0, dims[axis]) for axis in range(len(dims))]
    drawn = drawn.at[tuple(index_at)].set(low)
    longest = dims.index(max(dims))
    index_at[longest] = (index_at[longest] + 1) % dims[longest]
    return drawn.at[tuple(index_at)].set(largest)


def block_scale(rng, shape, shards, least, largest):
    loudness, own = 1.0, jax.random.fold_in(rng, 6)
    for axis_at, blocks in shards:
        draws = jnp.exp(jax.random.uniform(jax.random.fold_in(own, axis_at), (blocks,), jnp.float32, least / len(shards), largest / len(shards)))
        loudness = loudness * jnp.repeat(draws, shape[axis_at] // blocks).reshape([-1 if axis == axis_at else 1 for axis in range(len(shape))])
    return loudness


def gaussian(own_key, extent, deviation, limit, cuts=(), held_as=jnp.bfloat16):
    values = jax.random.normal(own_key, extent, jnp.float32) * deviation
    if len(cuts) > 0:
        values = block_scale(own_key, extent, cuts, -0.22, 0.18) * values
    return jnp.clip(values, min=-limit, max=limit).astype(held_as)


def setup_inputs(seed: int = 0) -> dict:
    arg_keys = jax.random.split(jax.random.key(seed), 12)
    return {
        "atm_state": gaussian(arg_keys[0], (NV, LEV, COLUMNS), 1.0, 6.0, ((2, 128),), jnp.float32),
        "diffusivity": jnp.clip(jnp.exp(math.log(10.0) - 4.6051702 * jax.random.uniform(arg_keys[1], (LEV - 1, COLUMNS), jnp.float32) ** block_scale(arg_keys[1], (LEV - 1, COLUMNS), ((1, 128),), -0.2, 0.2)), 0.1, 10.0),
        "send_slot": draw_send_slot(jax.random.fold_in(arg_keys[11], 71), 0),
        "atm_block": set_ends(jax.random.randint(arg_keys[3], (DEVICES, NBLK), 0, ABLK), jax.random.fold_in(arg_keys[3], 1), 0, ABLK - 1).astype(jnp.int32),
        "recv_row": draw_recv_row(jax.random.fold_in(arg_keys[11], 71), 0),
        "remap_weight": jnp.clip(0.001953125 * jax.random.uniform(arg_keys[5], (DEVICES * NBLK, ORX, ORX), jnp.float32) ** block_scale(arg_keys[5], (DEVICES * NBLK, ORX, ORX), ((0, 128),), -0.2, 0.2), 0.0, 0.001953125).astype(jnp.bfloat16),
        "ocean_tracer": gaussian(arg_keys[6], (NV, OLEV, NY_O, NX_O), 1.0, 6.0, ((2, 16), (3, 8)), jnp.float32),
        "ocean_velocity": jnp.clip(jax.random.uniform(arg_keys[7], (2, OLEV, NY_O, NX_O), jnp.float32, -0.24, 0.24) * block_scale(arg_keys[7], (2, OLEV, NY_O, NX_O), ((2, 16), (3, 8)), -0.4, 0.0), -0.24, 0.24),
        "exchange_coef": jnp.clip(jnp.exp(math.log(5.0) - 3.218876 * jax.random.uniform(arg_keys[8], (NY_O, NX_O), jnp.float32) ** block_scale(arg_keys[8], (NY_O, NX_O), ((0, 16), (1, 8)), -0.2, 0.2)), 0.2, 5.0),
        "surface_kind": set_ends(jax.random.randint(arg_keys[9], (NY_O, NX_O), 0, 3), jax.random.fold_in(arg_keys[9], 1), 0, 2).astype(jnp.int32),
        "ice_surface": gaussian(arg_keys[10], (NV, NY_O, NX_O), 1.0, 6.0, ((1, 16), (2, 8)), jnp.float32),
    }


def down_sweep(profile, diffusion):
    lev_count = profile.shape[1]
    coef_c = []
    coef_g = []
    recip_now = None
    for height in range(lev_count):
        denominator = jnp.ones_like(diffusion[0])
        right_side = profile[:, height]
        if height > 0:
            denominator = denominator + diffusion[height - 1] + diffusion[height - 1] * coef_c[-1]
            right_side = right_side + diffusion[height - 1] * coef_g[-1]
        if height < lev_count - 1:
            denominator = denominator + diffusion[height]
        recip_now = 1.0 / denominator
        coef_g.append(right_side * recip_now)
        if height < lev_count - 1:
            coef_c.append(-diffusion[height] * recip_now)
    return coef_c, coef_g, recip_now


def up_sweep(coef_c, coef_g, recip_now, surface_flux):
    column = coef_g[-1] + recip_now * surface_flux
    result = [column]
    for height in range(len(coef_c) - 1, -1, -1):
        column = coef_g[height] - coef_c[height] * column
        result.append(column)
    return jnp.stack(result[::-1], axis=1)


def advect(tracer, speed_rows, speed_cols):
    inner_rows = tracer[..., :, 1:-1]
    along_rows = speed_rows[:, :, 1:-1]
    face_rows = 0.5 * (along_rows[:, :-1] + along_rows[:, 1:])
    flow_rows = jnp.maximum(face_rows, 0.0) * inner_rows[..., :-1, :] + jnp.minimum(face_rows, 0.0) * inner_rows[..., 1:, :]
    inner_cols = tracer[..., 1:-1, :]
    along_cols = speed_cols[:, 1:-1, :]
    face_cols = 0.5 * (along_cols[..., :-1] + along_cols[..., 1:])
    flow_cols = jnp.maximum(face_cols, 0.0) * inner_cols[..., :-1] + jnp.minimum(face_cols, 0.0) * inner_cols[..., 1:]
    return tracer[..., 1:-1, 1:-1] - (flow_rows[..., 1:, :] - flow_rows[..., :-1, :]) - (flow_cols[..., 1:] - flow_cols[..., :-1])


def reference(atm_state, diffusivity, send_slot, atm_block, recv_row, remap_weight, ocean_tracer, ocean_velocity, exchange_coef, surface_kind, ice_surface):
    var_count = atm_state.shape[0]
    block_width = remap_weight.shape[1]
    devices = send_slot.shape[0]
    per_dev = send_slot.shape[1]
    fields = var_count + 1
    block_count = atm_state.shape[2] // devices // block_width
    coef_c, coef_g, recip_now = down_sweep(atm_state, diffusivity)
    packed = jnp.concatenate([coef_g[-1], recip_now[None]], axis=0).astype(jnp.bfloat16)
    by_device = packed.reshape(fields, devices, block_count, block_width).transpose(1, 2, 0, 3)
    weights = remap_weight.reshape(devices, per_dev, block_width, block_width)

    def forward(pieces):
        packed_dev, weight_dev, block_dev = pieces
        picked = jnp.take(packed_dev, block_dev, axis=0).astype(jnp.float32)
        return jnp.einsum('boa,bfa->bfo', weight_dev.astype(jnp.float32), picked)

    contrib = lax.map(forward, (by_device, weights, atm_block))
    owners = send_slot // CAP
    sources = jnp.arange(devices, dtype=jnp.int32)[:, None]
    rows_in = recv_row[owners, sources * CAP + send_slot % CAP]
    target = ((owners // N_OCN) * ORY + rows_in) * N_OCN + owners % N_OCN
    ocean_rows = ocean_tracer.shape[2]
    summed = jax.ops.segment_sum(contrib.reshape(-1, fields, block_width), target.reshape(-1), num_segments=ocean_rows * N_OCN)
    summed = summed.reshape(ocean_rows, N_OCN, fields, block_width).transpose(2, 0, 1, 3).reshape(fields, ocean_rows, -1)
    surface = jnp.where(surface_kind == 2, ice_surface, ocean_tracer[:, 0])
    coupling = jnp.where(surface_kind == 0, 0.0, exchange_coef)
    fluxes = coupling * (surface - summed[:var_count]) / (1.0 + coupling * summed[var_count])
    rounded = fluxes.astype(jnp.bfloat16)
    flux_rows = rounded.reshape(var_count, ocean_rows, N_OCN, block_width).transpose(1, 2, 0, 3).reshape(-1, var_count, block_width)

    def backward(pieces):
        weight_dev, target_dev, block_dev = pieces
        picked = jnp.take(flux_rows, target_dev, axis=0).astype(jnp.float32)
        spread = jnp.einsum('boa,bvo->bva', weight_dev.astype(jnp.float32), picked)
        return jax.ops.segment_sum(spread, block_dev, num_segments=block_count)

    returned = lax.map(backward, (weights, target, atm_block))
    surface_flux = returned.transpose(2, 0, 1, 3).reshape(var_count, -1)
    atm_new = up_sweep(coef_c, coef_g, recip_now, surface_flux)
    tracer = ocean_tracer.at[:, 0].add(-fluxes)
    padded_speed = jnp.pad(ocean_velocity, ((0, 0), (0, 0), (1, 1), (1, 1)))
    for substep in range(NSUB):
        padded = jnp.pad(tracer, ((0, 0), (0, 0), (1, 1), (1, 1)))
        tracer = advect(padded, padded_speed[0], padded_speed[1])
    return atm_new, tracer
```

```python
import functools
import jax
import jax.numpy as jnp
from jax import lax
from jax.experimental import pallas as pl
from jax.experimental.pallas import tpu as pltpu
from jax.sharding import PartitionSpec as P

F32, BF16, I32 = jnp.float32, jnp.bfloat16, jnp.int32
MESH = pl.DeviceIdType.MESH
VM = pl.BlockSpec(memory_space=pltpu.VMEM)
SM = pl.BlockSpec(memory_space=pltpu.SMEM)
ANY = pl.BlockSpec(memory_space=pl.ANY)
NV, LEV, NBLK, AB, SLOTS = 3, 63, 256, 16, 512
WCH = 8


def w_copies(w_hbm, w_ref, sem):
    n = NBLK // WCH
    return [pltpu.make_async_copy(w_hbm.at[pl.ds(i * n, n)], w_ref.at[pl.ds(i * n, n)], sem.at[i]) for i in range(WCH)]


def k1_body(slot_ref, ablk_ref, atm_ref, dif_ref, w_hbm, sb_ref, c_ref, g_ref, r_ref,
            w_ref, s_ref, d_ref, pk_ref, sl_ref, sem):
    cps = w_copies(w_hbm, w_ref, sem)
    for cp in cps:
        cp.start()
    for v in range(NV + 1):
        rows = LEV if v < NV else LEV - 1
        for i in range(8):
            n = min(8, rows - 8 * i)
            for j in range(16):
                src = atm_ref[v, pl.ds(8 * i, n), pl.ds(128 * j, 128)] if v < NV else dif_ref[pl.ds(8 * i, n), pl.ds(128 * j, 128)]
                if v < NV:
                    s_ref[pl.ds(v * 1024 + 8 * i * 16 + j, n, stride=16), :] = src
                else:
                    d_ref[pl.ds(8 * i * 16 + j, n, stride=16), :] = src
    sl_ref[...] = jnp.zeros_like(sl_ref)

    def level(k, kprev, know, c, g):
        den = 1.0 + kprev + know + kprev * c
        r = 1.0 / den
        gn = []
        for v in range(NV):
            gv = (s_ref[pl.ds(v * 1024 + k * 16, 16), :] + kprev * g[v]) * r
            g_ref[v, pl.ds(k * 16, 16), :] = gv
            gn.append(gv)
        return r, gn

    z = jnp.zeros((16, 128), F32)

    def step(k, carry):
        kprev, c, g = carry
        know = d_ref[pl.ds(k * 16, 16), :]
        r, gn = level(k, kprev, know, c, g)
        cn = -know * r
        c_ref[pl.ds(k * 16, 16), :] = cn
        return know, cn, gn

    kprev, c, g = lax.fori_loop(0, LEV - 1, step, (z, z, [z, z, z]), unroll=2)
    r, g = level(LEV - 1, kprev, z, c, g)
    r_ref[...] = r
    for f in range(4):
        val = g[f] if f < 3 else r
        pk_ref[pl.ds(f, 16, stride=8), :] = val
        pk_ref[pl.ds(f + 4, 16, stride=8), :] = val
    low = lax.broadcasted_iota(I32, (8, 128), 0) < 4
    for i in range(WCH):
        cps[i].wait()
        n = NBLK // WCH // 4

        def blocks(q, _):
            b = i * (NBLK // WCH) + q * 4
            xs = []
            for h in range(2):
                m0 = ablk_ref[b + 2 * h]
                m1 = ablk_ref[b + 2 * h + 1]
                x0 = pk_ref[pl.ds(pl.multiple_of(m0 * 8, 8), 8), :]
                x1 = pk_ref[pl.ds(pl.multiple_of(m1 * 8, 8), 8), :]
                xs.append(jnp.where(low, x0, x1))
            x = jnp.concatenate(xs, axis=0).astype(BF16)
            for h in range(2):
                w = w_ref[pl.ds(b + 2 * h, 2)].reshape(256, 128)
                y = lax.dot_general(x, w, (((1,), (1,)), ((), ())), preferred_element_type=F32)
                t0 = slot_ref[b + 2 * h]
                t1 = slot_ref[b + 2 * h + 1]
                sl_ref[pl.ds(t0 * 4, 4), :] = y[8 * h:8 * h + 4, 0:128]
                sl_ref[pl.ds(t1 * 4, 4), :] = y[8 * h + 4:8 * h + 8, 128:256]
            return 0

        lax.fori_loop(0, n, blocks, 0)
    sb_ref[...] = sl_ref[...].astype(BF16)


def k1(slot, ablk, atm, dif, w):
    return pl.pallas_call(
        k1_body,
        out_shape=(jax.ShapeDtypeStruct((2048, 128), BF16),
                   jax.ShapeDtypeStruct((1024, 128), F32),
                   jax.ShapeDtypeStruct((NV, 1024, 128), F32),
                   jax.ShapeDtypeStruct((16, 128), F32)),
        in_specs=[SM, SM, VM, VM, ANY],
        out_specs=(VM, VM, VM, VM),
        scratch_shapes=[pltpu.VMEM((NBLK, 128, 128), BF16), pltpu.VMEM((NV * 1024, 128), F32),
                        pltpu.VMEM((1024, 128), F32), pltpu.VMEM((128, 128), F32),
                        pltpu.VMEM((2048, 128), F32), pltpu.SemaphoreType.DMA((WCH,))],
        compiler_params=pltpu.CompilerParams(vmem_limit_bytes=40 << 20), name="down_forward",
    )(slot, ablk, atm, dif, w)


def k3_body(slot_ref, ablk_ref, ans_ref, w_hbm, c_ref, g_ref, r_ref, out_ref,
            w_ref, af_ref, acc_ref, x_ref, sem):
    cps = w_copies(w_hbm, w_ref, sem)
    for cp in cps:
        cp.start()
    af_ref[...] = ans_ref[...].astype(F32)
    acc_ref[...] = jnp.zeros_like(acc_ref)
    for i in range(WCH):
        cps[i].wait()
        n = NBLK // WCH // 4

        def blocks(q, _):
            b = i * (NBLK // WCH) + q * 4
            x = jnp.concatenate([af_ref[pl.ds(pl.multiple_of(slot_ref[b + h] * 4, 4), 4), :] for h in range(4)], axis=0).astype(BF16)
            for h in range(4):
                y = jnp.dot(x, w_ref[b + h], preferred_element_type=F32)
                m = pl.multiple_of(ablk_ref[b + h] * 8, 8)
                acc_ref[h, pl.ds(m, 4), :] = acc_ref[h, pl.ds(m, 4), :] + y[4 * h:4 * h + 4]
            return 0

        lax.fori_loop(0, n, blocks, 0)
    tot = acc_ref[0] + acc_ref[1] + acc_ref[2] + acc_ref[3]
    acc_ref[0] = tot
    r = r_ref[...]
    xs = []
    for v in range(NV):
        sf = acc_ref[0, pl.ds(v, 16, stride=8), :]
        x = g_ref[v, pl.ds((LEV - 1) * 16, 16), :] + r * sf
        x_ref[pl.ds(v * 1024 + (LEV - 1) * 16, 16), :] = x
        xs.append(x)

    def step(i, xs):
        k = LEV - 2 - i
        c = c_ref[pl.ds(k * 16, 16), :]
        new = []
        for v in range(NV):
            x = g_ref[v, pl.ds(k * 16, 16), :] - c * xs[v]
            x_ref[pl.ds(v * 1024 + k * 16, 16), :] = x
            new.append(x)
        return new

    lax.fori_loop(0, LEV - 1, step, xs, unroll=2)
    for v in range(NV):
        for i in range(8):
            n = min(8, LEV - 8 * i)
            for j in range(16):
                out_ref[v, pl.ds(8 * i, n), pl.ds(128 * j, 128)] = x_ref[pl.ds(v * 1024 + 8 * i * 16 + j, n, stride=16), :]


def k3(slot, ablk, ans, w, c, g, r):
    return pl.pallas_call(
        k3_body,
        out_shape=jax.ShapeDtypeStruct((NV, LEV, 2048), F32),
        in_specs=[SM, SM, VM, ANY, VM, VM, VM],
        out_specs=VM,
        scratch_shapes=[pltpu.VMEM((NBLK, 128, 128), BF16), pltpu.VMEM((2048, 128), F32),
                        pltpu.VMEM((4, 128, 128), F32), pltpu.VMEM((NV * 1024, 128), F32),
                        pltpu.SemaphoreType.DMA((WCH,))],
        compiler_params=pltpu.CompilerParams(vmem_limit_bytes=40 << 20), name="backward_up",
    )(slot, ablk, ans, w, c, g, r)

NDEV, OL, PH = 128, 75, 48
PLANES = 228
NROW = 304
NTILE = 6


def rk_body(sb_ref, val_ref, tr_hbm, ve_hbm, hx_ref, kind_ref, ice_ref, ans_ref, oc_hbm,
            tb, cb, ub, u1, er, hr, ec, hc, xc, er0, hr0, ec0, hc0, arr, rb, sel,
            lsem, osem, hs, hrs, hs0, hr0s, asem):
    A = lax.axis_index("atm")
    O = lax.axis_index("ocn")
    me = A * 8 + O

    def dev(d):
        return (d // 8, lax.rem(d, 8))

    loads = []
    tb4 = tb.reshape(PLANES // 3, 3, PH, 128)
    ub3 = ub.reshape(80, PH, 128)
    for v in range(3):
        loads.append(pltpu.make_async_copy(tr_hbm.at[v], tb4.at[pl.ds(0, OL), v, pl.ds(8, 32)], lsem.at[v]))
    loads.append(pltpu.make_async_copy(ve_hbm.at[0], ub3.at[pl.ds(0, OL), pl.ds(8, 32)], lsem.at[3]))
    loads.append(pltpu.make_async_copy(ve_hbm.at[1], u1, lsem.at[4]))
    for cp in loads:
        cp.start()

    bar = pltpu.get_barrier_semaphore()

    def sig(i, _):
        pl.semaphore_signal(bar, inc=1, device_id=dev(lax.rem(me + i, NDEV)), device_id_type=MESH)
        return 0

    lax.fori_loop(1, NDEV, sig, 0)

    lane = lax.broadcasted_iota(I32, (32, 128), 1)
    mn = jnp.where(A > 0, 1.0, 0.0).astype(F32)
    ms = jnp.where(A < 15, 1.0, 0.0).astype(F32)
    mw = jnp.where(O > 0, 1.0, 0.0).astype(F32)
    mx = jnp.where(O < 7, 1.0, 0.0).astype(F32)

    sel[...] = jnp.where(val_ref[...] == lax.broadcasted_iota(I32, (128, 2048), 0), 1.0, 0.0).astype(BF16)
    tb[pl.ds(OL * 3 * PH, 3 * PH), :] = jnp.zeros((3 * PH, 128), F32)
    ub[pl.ds(OL * PH, 5 * PH), :] = jnp.zeros((5 * PH, 128), F32)
    ec[...] = jnp.zeros_like(ec)
    ec0[...] = jnp.zeros_like(ec0)
    for cp in loads:
        cp.wait()

    def pack_rows(k):
        def g(i, _):
            for side, row in ((0, 8), (1, 39)):
                er[k, side, pl.ds(pl.multiple_of(i * 8, 8), 8), :] = tb[pl.ds((3 + 8 * i) * PH + row, 8, stride=PH), :]
            return 0
        lax.fori_loop(0, 28, g, 0, unroll=4)

    def unpack_rows(k):
        def g(i, _):
            for side, row, m in ((0, 7, mn), (1, 40, ms)):
                tb[pl.ds((3 + 8 * i) * PH + row, 8, stride=PH), :] = hr[k, side, pl.ds(pl.multiple_of(i * 8, 8), 8), :] * m
            return 0
        lax.fori_loop(0, 28, g, 0, unroll=4)

    def edge(x, sh):
        return pltpu.roll(x, lax.rem(sh + 1, 128), 1)

    def put(ref_view, val, lo, n):
        pltpu.store(ref_view, val, mask=(lane >= lo) & (lane < lo + n))

    def three(vals, lo):
        ro = [edge(vals[v], lo + 2 * v) for v in range(3)]
        return jnp.where(lane < lo + 2, ro[0], jnp.where(lane < lo + 4, ro[1], ro[2]))

    def merge(w, e):
        return jnp.where(lax.rem(lane, 2) == 0, w * mw, pltpu.roll(e, 126, 1) * mx)

    def row_at(p):
        return pl.multiple_of(p * PH + 8, 8)

    def uedge(i, _):
        for side, row in ((0, 8), (1, 39)):
            er[0, side, pl.ds(pl.multiple_of(224 + i * 8, 8), 8), :] = ub[pl.ds(8 * i * PH + row, 8, stride=PH), :]
        return 0

    lax.fori_loop(0, 10, uedge, 0, unroll=2)
    pack_rows(0)

    def cedge(l, _):
        i = l - 1
        lo = lax.rem(i, 21) * 6
        vals = [tb[pl.ds(row_at(l * 3 + v), 32), :] for v in range(3)]
        put(ec.at[0, i // 21], three(vals, lo), lo, 6)
        return 0

    lax.fori_loop(1, OL, cedge, 0)

    def vedge(l, _):
        lo = lax.rem(l, 64) * 2
        put(ec.at[0, 4 + l // 64], edge(u1[l], lo), lo, 2)
        return 0

    lax.fori_loop(0, OL, vedge, 0)

    def halo(k):
        n = NROW if k == 0 else 224
        t = NTILE if k == 0 else 4
        up = (lax.rem(A + 15, 16), O)
        down = (lax.rem(A + 1, 16), O)
        west = (A, lax.rem(O + 7, 8))
        east = (A, lax.rem(O + 1, 8))
        mk = pltpu.make_async_remote_copy
        rows = pl.ds(0, n)
        tiles = pl.ds(0, t)
        return [
            mk(er.at[k, 0, rows], hr.at[k, 1, rows], hs.at[k, 0], hrs.at[k, 0], device_id=up, device_id_type=MESH),
            mk(er.at[k, 1, rows], hr.at[k, 0, rows], hs.at[k, 1], hrs.at[k, 1], device_id=down, device_id_type=MESH),
            mk(ec.at[k, tiles], hc.at[k, 1, tiles], hs.at[k, 2], hrs.at[k, 2], device_id=west, device_id_type=MESH),
            mk(ec.at[k, tiles], hc.at[k, 0, tiles], hs.at[k, 3], hrs.at[k, 3], device_id=east, device_id_type=MESH),
        ]

    def halo0(k):
        up = (lax.rem(A + 15, 16), O)
        down = (lax.rem(A + 1, 16), O)
        west = (A, lax.rem(O + 7, 8))
        east = (A, lax.rem(O + 1, 8))
        mk = pltpu.make_async_remote_copy
        return [
            mk(er0.at[k, 0], hr0.at[k, 1], hs0.at[k, 0], hr0s.at[k, 0], device_id=up, device_id_type=MESH),
            mk(er0.at[k, 1], hr0.at[k, 0], hs0.at[k, 1], hr0s.at[k, 1], device_id=down, device_id_type=MESH),
            mk(ec0.at[k], hc0.at[k, 1], hs0.at[k, 2], hr0s.at[k, 2], device_id=west, device_id_type=MESH),
            mk(ec0.at[k], hc0.at[k, 0], hs0.at[k, 3], hr0s.at[k, 3], device_id=east, device_id_type=MESH),
        ]

    pl.semaphore_wait(bar, NDEV - 1)
    H = [halo(k) for k in range(4)]
    H0 = [halo0(k) for k in range(4)]

    def start(cs):
        for cp in cs:
            cp.start()

    def arrive(cs):
        for cp in cs:
            cp.wait_recv()

    def send_all(src, dst, ssem, rsem):
        def f(i, _):
            d = lax.rem(me + i, NDEV)
            pltpu.make_async_remote_copy(src.at[d], dst.at[me], ssem, rsem, device_id=dev(d), device_id_type=MESH).start()
            return 0
        lax.fori_loop(1, NDEV, f, 0)

    def bulk(ref, sem):
        pltpu.make_async_copy(ref.at[pl.ds(0, NDEV - 1)], ref.at[pl.ds(0, NDEV - 1)], sem).wait()

    send_all(sb_ref, arr, asem.at[0], asem.at[1])
    start(H[0])
    own = pltpu.make_async_copy(sb_ref.at[me], arr.at[me], asem.at[4])
    own.start()

    def tiles_in(k):
        for t in range(4):
            xc[t] = merge(hc[k, 0, t], hc[k, 1, t])

    def advance(l, xt, lo, k):
        co = [cb[pl.ds(pl.multiple_of((l * 5 + j) * 32, 8), 32), :] for j in range(5)]
        vals = []
        for v in range(3):
            base = (l * 3 + v) * PH
            t = tb[pl.ds(pl.multiple_of(base + 8, 8), 32), :]
            tn = tb[pl.ds(base + 7, 32), :]
            ts = tb[pl.ds(base + 9, 32), :]
            h = pltpu.roll(xt, lax.rem(128 - (lo + 2 * v), 128), 1)
            tw = jnp.where(lane == 0, h, pltpu.roll(t, 1, 1))
            te = jnp.where(lane == 127, h, pltpu.roll(t, 127, 1))
            new = co[0] * t + co[1] * tn + co[2] * ts + co[3] * tw + co[4] * te
            tb[pl.ds(pl.multiple_of(base + 8, 8), 32), :] = new
            vals.append(new)
        return vals

    def main_round(k):
        def f(l, _):
            i = l - 1
            tile = i // 21
            lo = lax.rem(i, 21) * 6
            vals = advance(l, xc[tile], lo, k)
            if k < 3:
                put(ec.at[k + 1, tile], three(vals, lo), lo, 6)
            return 0
        lax.fori_loop(1, OL, f, 0)

    def coefs():
        xv = [merge(hc[0, 0, 4 + t], hc[0, 1, 4 + t]) for t in range(2)]
        xc[4] = xv[0]
        xc[5] = xv[1]

        def hrow(i, _):
            for side, row, m in ((0, 7, mn), (1, 40, ms)):
                ub[pl.ds(8 * i * PH + row, 8, stride=PH), :] = hr[0, side, pl.ds(pl.multiple_of(224 + i * 8, 8), 8), :] * m
            return 0

        lax.fori_loop(0, 10, hrow, 0, unroll=2)

        def f(l, _):
            base = l * PH
            a = ub[pl.ds(pl.multiple_of(base + 8, 8), 32), :]
            fn = 0.5 * (ub[pl.ds(base + 7, 32), :] + a)
            fs = 0.5 * (a + ub[pl.ds(base + 9, 32), :])
            b = u1[l]
            h = pltpu.roll(xc[4 + l // 64], lax.rem(128 - lax.rem(l, 64) * 2, 128), 1)
            fw = 0.5 * (jnp.where(lane == 0, h, pltpu.roll(b, 1, 1)) + b)
            fe = 0.5 * (b + jnp.where(lane == 127, h, pltpu.roll(b, 127, 1)))
            zero = jnp.zeros_like(a)
            mid = 1.0 - jnp.maximum(fs, zero) + jnp.minimum(fn, zero) - jnp.maximum(fe, zero) + jnp.minimum(fw, zero)
            outs = (mid, jnp.maximum(fn, zero), -jnp.minimum(fs, zero), jnp.maximum(fw, zero), -jnp.minimum(fe, zero))
            for j in range(5):
                cb[pl.ds(pl.multiple_of((l * 5 + j) * 32, 8), 32), :] = outs[j]
            return 0

        lax.fori_loop(0, OL, f, 0)

    def send_main(k):
        pack_rows(k)
        start(H[k])

    def recv_main(k):
        arrive(H[k])
        unpack_rows(k)
        tiles_in(k)

    recv_main(0)
    coefs()
    main_round(0)
    send_main(1)
    recv_main(1)
    main_round(1)
    send_main(2)

    own.wait()
    bulk(arr, asem.at[1])
    summed = jnp.dot(sel[...], arr[...].reshape(2048, 128), preferred_element_type=F32)
    h = jnp.where(kind_ref[...] == 0, 0.0, hx_ref[...])
    den = 1.0 + h * summed[96:128]
    zb = jnp.zeros((32, 128), BF16)
    parts = []
    forced = []
    for v in range(3):
        t0 = tb[pl.ds(v * PH + 8, 32), :]
        surf = jnp.where(kind_ref[...] == 2, ice_ref[v], t0)
        flux = h * (surf - summed[32 * v:32 * v + 32]) / den
        parts.append(flux.astype(BF16))
        t0 = t0 - flux
        tb[pl.ds(v * PH + 8, 32), :] = t0
        forced.append(t0)
    fb = jnp.concatenate(parts + [zb], axis=0)
    ret = lax.dot_general(sel[...], fb, (((0,), (0,)), ((), ())), preferred_element_type=F32)
    rb[...] = ret.astype(BF16).reshape(NDEV, 16, 128)
    send_all(rb, ans_ref, asem.at[2], asem.at[3])
    own2 = pltpu.make_async_copy(rb.at[me], ans_ref.at[me], asem.at[5])
    own2.start()

    def send_zero(k, vals):
        for side, row in ((0, 8), (1, 39)):
            er0[k, side, :, :] = tb[pl.ds(row, 8, stride=PH), :]
        ec0[k] = three(vals, 0)
        start(H0[k])

    def recv_zero(k):
        arrive(H0[k])
        for side, row, m in ((0, 7, mn), (1, 40, ms)):
            tb[pl.ds(row, 3, stride=PH), :] = hr0[k, side, 0:3, :] * m
        return advance(0, merge(hc0[k, 0], hc0[k, 1]), 0, k)

    send_zero(0, forced)
    recv_main(2)
    main_round(2)
    send_main(3)
    send_zero(1, recv_zero(0))
    recv_main(3)
    main_round(3)
    outs = [pltpu.make_async_copy(tb4.at[pl.ds(1, OL - 1), v, pl.ds(8, 32)], oc_hbm.at[v, pl.ds(1, OL - 1)], osem.at[v]) for v in range(3)]
    start(outs)
    send_zero(2, recv_zero(1))
    send_zero(3, recv_zero(2))
    recv_zero(3)
    outs0 = [pltpu.make_async_copy(tb4.at[0, v, pl.ds(8, 32)], oc_hbm.at[v, 0], osem.at[3 + v]) for v in range(3)]
    start(outs0)
    own2.wait()
    bulk(ans_ref, asem.at[3])
    bulk(sb_ref, asem.at[0])
    bulk(rb, asem.at[2])
    for cs in H + H0:
        for cp in cs:
            cp.wait_send()
    for cp in outs + outs0:
        cp.wait()


def rk(sb, val, tracer, velocity, hx, kind, ice):
    D = pltpu.SemaphoreType.DMA
    V = pltpu.VMEM
    return pl.pallas_call(
        rk_body,
        out_shape=(jax.ShapeDtypeStruct((NDEV, 16, 128), BF16), jax.ShapeDtypeStruct((3, OL, 32, 128), F32)),
        in_specs=[VM, VM, ANY, ANY, VM, VM, VM],
        out_specs=(VM, ANY),
        scratch_shapes=[
            V((PLANES * PH, 128), F32), V((OL * 5 * 32, 128), F32), V((80 * PH, 128), F32), V((OL, 32, 128), F32),
            V((4, 2, NROW, 128), F32), V((4, 2, NROW, 128), F32),
            V((4, NTILE, 32, 128), F32), V((4, 2, NTILE, 32, 128), F32), V((NTILE, 32, 128), F32),
            V((4, 2, 8, 128), F32), V((4, 2, 8, 128), F32), V((4, 32, 128), F32), V((4, 2, 32, 128), F32),
            V((NDEV, 16, 128), BF16), V((NDEV, 16, 128), BF16), V((128, 2048), BF16),
            D((5,)), D((6,)), D((4, 4)), D((4, 4)), D((4, 4)), D((4, 4)), D((6,)),
        ],
        compiler_params=pltpu.CompilerParams(collective_id=0, has_side_effects=True, vmem_limit_bytes=48 << 20),
        name="exchange_ocean",
    )(sb, val, tracer, velocity, hx, kind, ice)

def per_device(atm_state, diffusivity, send_slot, atm_block, recv_row, remap_weight, ocean_tracer, ocean_velocity,
               exchange_coef, surface_kind, ice_surface):
    slot, ablk = send_slot[0], atm_block[0]
    sb, c, g, r = k1(slot, ablk, atm_state, diffusivity, remap_weight)
    lanes = jnp.arange(2048, dtype=I32)
    rr = jnp.repeat(recv_row[0], 4)
    val = jnp.where(rr >= 0, rr + 32 * (lanes % 4), -1)[None, :]
    ans, ocean = rk(sb.reshape(128, 16, 128), val, ocean_tracer, ocean_velocity, exchange_coef, surface_kind, ice_surface)
    atm_new = k3(slot, ablk, ans.reshape(2048, 128), remap_weight, c, g, r)
    return atm_new, ocean


def solution(mesh):
    placed = (
        P(None, None, ("atm", "ocn")),
        P(None, ("atm", "ocn")),
        P(("atm", "ocn"), None),
        P(("atm", "ocn"), None),
        P(("atm", "ocn"), None),
        P(("atm", "ocn"), None, None),
        P(None, None, "atm", "ocn"),
        P(None, None, "atm", "ocn"),
        P("atm", "ocn"),
        P("atm", "ocn"),
        P(None, "atm", "ocn"),
    )
    return jax.shard_map(
        per_device,
        mesh=mesh,
        in_specs=placed,
        out_specs=(P(None, None, ("atm", "ocn")), P(None, None, "atm", "ocn")),
        check_vma=False,
    )
```

```python
import functools
import jax
import jax.numpy as jnp
from jax import lax
from jax.experimental import pallas as pl
from jax.experimental.pallas import tpu as pltpu
from jax.sharding import PartitionSpec as P

F32, BF16, I32 = jnp.float32, jnp.bfloat16, jnp.int32
MESH = pl.DeviceIdType.MESH
VM = pl.BlockSpec(memory_space=pltpu.VMEM)
SM = pl.BlockSpec(memory_space=pltpu.SMEM)
ANY = pl.BlockSpec(memory_space=pltpu.HBM)
NV, LEV, NBLK, AB, SLOTS = 3, 63, 256, 16, 512
WCH = 16


def w_copy(w_hbm, w_ref, sem, i):
    n = NBLK // WCH
    rows = pl.ds(i * n, n)
    return pltpu.make_async_copy(w_hbm.at[rows], w_ref.at[rows], sem.at[i])


def w_copies(w_hbm, w_ref, sem):
    return [w_copy(w_hbm, w_ref, sem, i) for i in range(WCH)]


def k1_body(slot_ref, ablk_ref, atm_hbm, dif_hbm, w_hbm, sb_ref, c_ref, g_ref, r_ref,
            w_ref, atm_ref, dif_ref, s_ref, d_ref, pk_ref, sl_ref, sem, isem):
    ins = [pltpu.make_async_copy(atm_hbm, atm_ref, isem.at[0]), pltpu.make_async_copy(dif_hbm, dif_ref, isem.at[1])]
    cps = w_copies(w_hbm, w_ref, sem)
    for cp in ins + cps:
        cp.start()
    sl_ref[...] = jnp.zeros_like(sl_ref)
    for cp in ins:
        cp.wait()
    for v in range(NV + 1):
        rows = LEV if v < NV else LEV - 1
        for i in range(8):
            n = min(8, rows - 8 * i)
            for j in range(16):
                src = atm_ref[v, pl.ds(8 * i, n), pl.ds(128 * j, 128)] if v < NV else dif_ref[pl.ds(8 * i, n), pl.ds(128 * j, 128)]
                if v < NV:
                    s_ref[pl.ds(v * 1024 + 8 * i * 16 + j, n, stride=16), :] = src
                else:
                    d_ref[pl.ds(8 * i * 16 + j, n, stride=16), :] = src

    def level(k, kprev, know, c, g):
        den = 1.0 + kprev + know + kprev * c
        r = 1.0 / den
        gn = []
        for v in range(NV):
            gv = (s_ref[pl.ds(v * 1024 + k * 16, 16), :] + kprev * g[v]) * r
            g_ref[v, pl.ds(k * 16, 16), :] = gv
            gn.append(gv)
        return r, gn

    z = jnp.zeros((16, 128), F32)

    def step(k, carry):
        kprev, c, g = carry
        know = d_ref[pl.ds(k * 16, 16), :]
        r, gn = level(k, kprev, know, c, g)
        cn = -know * r
        c_ref[pl.ds(k * 16, 16), :] = cn
        return know, cn, gn

    kprev, c, g = lax.fori_loop(0, LEV - 1, step, (z, z, [z, z, z]), unroll=2)
    r, g = level(LEV - 1, kprev, z, c, g)
    r_ref[...] = r
    for f in range(4):
        val = g[f] if f < 3 else r
        pk_ref[pl.ds(f, 16, stride=8), :] = val
        pk_ref[pl.ds(f + 4, 16, stride=8), :] = val
    low = lax.broadcasted_iota(I32, (8, 128), 0) < 4

    def chunk(i, _):
        w_copy(w_hbm, w_ref, sem, i).wait()
        b = i * 16
        ys = []
        for q in range(4):
            xs = []
            for h in range(2):
                m0 = ablk_ref[b + 4 * q + 2 * h]
                m1 = ablk_ref[b + 4 * q + 2 * h + 1]
                x0 = pk_ref[pl.ds(pl.multiple_of(m0 * 8, 8), 8), :]
                x1 = pk_ref[pl.ds(pl.multiple_of(m1 * 8, 8), 8), :]
                xs.append(jnp.where(low, x0, x1).astype(BF16))
            for h in range(2):
                w = w_ref[pl.ds(b + 4 * q + 2 * h, 2)].reshape(256, 128)
                ys.append(lax.dot_general(xs[h], w, (((1,), (1,)), ((), ())), preferred_element_type=F32))
        for j in range(8):
            t0 = slot_ref[b + 2 * j]
            t1 = slot_ref[b + 2 * j + 1]
            sl_ref[pl.ds(t0 * 4, 4), :] = ys[j][0:4, 0:128]
            sl_ref[pl.ds(t1 * 4, 4), :] = ys[j][4:8, 128:256]
        return 0

    lax.fori_loop(0, WCH, chunk, 0)
    sb_ref[...] = sl_ref[...].astype(BF16)


def k1(slot, ablk, atm, dif, w):
    return pl.pallas_call(
        k1_body,
        out_shape=(jax.ShapeDtypeStruct((2048, 128), BF16),
                   jax.ShapeDtypeStruct((1024, 128), F32),
                   jax.ShapeDtypeStruct((NV, 1024, 128), F32),
                   jax.ShapeDtypeStruct((16, 128), F32)),
        in_specs=[SM, SM, ANY, ANY, ANY],
        out_specs=(VM, VM, VM, VM),
        scratch_shapes=[pltpu.VMEM((NBLK, 128, 128), BF16), pltpu.VMEM((NV, LEV, 2048), F32), pltpu.VMEM((LEV - 1, 2048), F32),
                        pltpu.VMEM((NV * 1024, 128), F32), pltpu.VMEM((1024, 128), F32), pltpu.VMEM((128, 128), F32),
                        pltpu.VMEM((2048, 128), F32), pltpu.SemaphoreType.DMA((WCH,)), pltpu.SemaphoreType.DMA((2,))],
        compiler_params=pltpu.CompilerParams(vmem_limit_bytes=62 << 20), name="down_forward",
    )(slot, ablk, atm, dif, w)


def k3_body(slot_ref, ablk_ref, ans_ref, w_hbm, c_hbm, g_hbm, r_ref, oc_in, out_hbm, oc_out,
            w_ref, c_ref, g_ref, oc_ref, af_ref, acc_ref, x_ref, out_ref, sem, isem, osem):
    cps = w_copies(w_hbm, w_ref, sem)
    ins = [pltpu.make_async_copy(c_hbm, c_ref, isem.at[0]), pltpu.make_async_copy(g_hbm, g_ref, isem.at[1])]
    oin = pltpu.make_async_copy(oc_in, oc_ref, isem.at[2])
    oout = pltpu.make_async_copy(oc_ref, oc_out, isem.at[3])
    for cp in cps + ins:
        cp.start()
    oin.start()
    af_ref[...] = ans_ref[...].astype(F32)
    acc_ref[...] = jnp.zeros_like(acc_ref)
    zero = jnp.zeros((4, 128), F32)

    def chunk(i, _):
        w_copy(w_hbm, w_ref, sem, i).wait()
        b = i * 16
        ys = []
        for q in range(8):
            x0 = af_ref[pl.ds(pl.multiple_of(slot_ref[b + 2 * q] * 4, 4), 4), :]
            x1 = af_ref[pl.ds(pl.multiple_of(slot_ref[b + 2 * q + 1] * 4, 4), 4), :]
            top = jnp.concatenate([x0, zero], axis=0)
            bot = jnp.concatenate([zero, x1], axis=0)
            x = jnp.concatenate([top, bot], axis=1).astype(BF16)
            ys.append(jnp.dot(x, w_ref[pl.ds(b + 2 * q, 2)].reshape(256, 128), preferred_element_type=F32))
        for j in range(16):
            m = pl.multiple_of(ablk_ref[b + j] * 8, 8)
            e = j % 2
            acc_ref[j % 8, pl.ds(m, 4), :] = acc_ref[j % 8, pl.ds(m, 4), :] + ys[j // 2][4 * e:4 * e + 4]
        return 0

    lax.fori_loop(0, WCH, chunk, 0)
    tot = acc_ref[0]
    for j in range(1, 8):
        tot = tot + acc_ref[j]
    acc_ref[0] = tot
    for cp in ins:
        cp.wait()
    oin.wait()
    oout.start()
    r = r_ref[...]
    xs = []
    for v in range(NV):
        sf = acc_ref[0, pl.ds(v, 16, stride=8), :]
        x = g_ref[v, pl.ds((LEV - 1) * 16, 16), :] + r * sf
        x_ref[pl.ds(v * 1024 + (LEV - 1) * 16, 16), :] = x
        xs.append(x)

    def down(k, xs):
        c = c_ref[pl.ds(k * 16, 16), :]
        new = []
        for v in range(NV):
            x = g_ref[v, pl.ds(k * 16, 16), :] - c * xs[v]
            x_ref[pl.ds(v * 1024 + k * 16, 16), :] = x
            new.append(x)
        return new

    def rows_out(i, n):
        for v in range(NV):
            for j in range(16):
                out_ref[v, pl.ds(8 * i, n), pl.ds(128 * j, 128)] = x_ref[pl.ds(v * 1024 + 8 * i * 16 + j, n, stride=16), :]

    for k in range(LEV - 2, 55, -1):
        xs = down(k, xs)
    rows_out(7, 7)

    def group(q, xs):
        i = 6 - q
        for d in range(8):
            xs = down(8 * i + 7 - d, xs)
        rows_out(i, 8)
        return xs

    lax.fori_loop(0, 7, group, xs)
    res = pltpu.make_async_copy(out_ref, out_hbm, osem)
    res.start()
    oout.wait()
    res.wait()


def k3(slot, ablk, ans, w, c, g, r, ocean):
    V = pltpu.VMEM
    return pl.pallas_call(
        k3_body,
        out_shape=(jax.ShapeDtypeStruct((NV, LEV, 2048), F32), jax.ShapeDtypeStruct((3, 75, 32, 128), F32)),
        in_specs=[SM, SM, VM, ANY, ANY, ANY, VM, ANY],
        out_specs=(ANY, ANY),
        scratch_shapes=[V((NBLK, 128, 128), BF16), V((1024, 128), F32), V((NV, 1024, 128), F32), V((3, 75, 32, 128), F32),
                        V((2048, 128), F32), V((8, 128, 128), F32), V((NV * 1024, 128), F32), V((NV, LEV, 2048), F32),
                        pltpu.SemaphoreType.DMA((WCH,)), pltpu.SemaphoreType.DMA((4,)), pltpu.SemaphoreType.DMA],
        compiler_params=pltpu.CompilerParams(vmem_limit_bytes=62 << 20), name="backward_up",
    )(slot, ablk, ans, w, c, g, r, ocean)

NDEV, OL, PH = 128, 75, 48
PLANES = 228
GROUPS = ((3, 15, 0, 20), (123, 13, 20, 37))


def rk_body(sb_ref, val_ref, tr_hbm, ve_hbm, hx_hbm, kind_hbm, ice_hbm, ans_ref, oc_hbm,
            hx_ref, kind_ref, ice_ref, tb, cb, ub, u1, er, hr, ec, hc, ev, hv, cv, hcv, xc, er0, hr0, ec0, hc0, arr, rb, sel,
            lsem, osem, hs, hrs, hsv, hrv, hs0, hr0s, asem):
    A = lax.axis_index("atm")
    O = lax.axis_index("ocn")
    me = A * 8 + O

    loads = []
    tb4 = tb.reshape(PLANES // 3, 3, PH, 128)
    ub3 = ub.reshape(80, PH, 128)
    for v in range(3):
        loads.append(pltpu.make_async_copy(tr_hbm.at[v], tb4.at[pl.ds(0, OL), v, pl.ds(8, 32)], lsem.at[v]))
    loads.append(pltpu.make_async_copy(ve_hbm.at[0], ub3.at[pl.ds(0, OL), pl.ds(8, 32)], lsem.at[3]))
    loads.append(pltpu.make_async_copy(ve_hbm.at[1], u1, lsem.at[4]))
    for i, (a, b) in enumerate(((hx_hbm, hx_ref), (kind_hbm, kind_ref), (ice_hbm, ice_ref))):
        loads.append(pltpu.make_async_copy(a, b, lsem.at[5 + i]))
    for cp in loads:
        cp.start()

    bar = pltpu.get_barrier_semaphore()

    cols = [lax.rem(O + j, 8) for j in range(8)]

    def to_all(fn):
        for j in range(1, 8):
            fn(A, cols[j])

        def f(i, _):
            a = lax.rem(A + i, 16)
            for j in range(8):
                fn(a, cols[j])
            return 0

        lax.fori_loop(1, 16, f, 0)

    to_all(lambda a, o: pl.semaphore_signal(bar, inc=1, device_id=(a, o), device_id_type=MESH))

    lane = lax.broadcasted_iota(I32, (32, 128), 1)
    mn = jnp.where(A > 0, 1.0, 0.0).astype(F32)
    ms = jnp.where(A < 15, 1.0, 0.0).astype(F32)
    mw = jnp.where(O > 0, 1.0, 0.0).astype(F32)
    mx = jnp.where(O < 7, 1.0, 0.0).astype(F32)

    sel[...] = jnp.where(val_ref[...] == lax.broadcasted_iota(I32, (128, 2048), 0), 1.0, 0.0).astype(BF16)
    tb[pl.ds(OL * 3 * PH, 3 * PH), :] = jnp.zeros((3 * PH, 128), F32)
    ub[pl.ds(OL * PH, 5 * PH), :] = jnp.zeros((5 * PH, 128), F32)
    ec[...] = jnp.zeros_like(ec)
    cv[...] = jnp.zeros_like(cv)
    ec0[...] = jnp.zeros_like(ec0)
    for cp in loads:
        cp.wait()

    def pack_rows(k, g):
        p0, n = GROUPS[g][:2]

        def f(i, _):
            for side, row in ((0, 8), (1, 39)):
                er[k, g, side, pl.ds(pl.multiple_of(i * 8, 8), 8), :] = tb[pl.ds((p0 + 8 * i) * PH + row, 8, stride=PH), :]
            return 0
        lax.fori_loop(0, n, f, 0)

    def unpack_rows(k, g):
        p0, n = GROUPS[g][:2]

        def f(i, _):
            for side, row, m in ((0, 7, mn), (1, 40, ms)):
                tb[pl.ds((p0 + 8 * i) * PH + row, 8, stride=PH), :] = hr[k, g, side, pl.ds(pl.multiple_of(i * 8, 8), 8), :] * m
            return 0
        lax.fori_loop(0, n, f, 0)

    def edge(x, sh):
        return pltpu.roll(x, sh + 1, 1)

    def put(ref_view, val, lo, n):
        pltpu.store(ref_view, val, mask=(lane >= lo) & (lane < lo + n))

    def three(vals, lo):
        ro = [edge(vals[v], lo + 2 * v) for v in range(3)]
        return jnp.where(lane < lo + 2, ro[0], jnp.where(lane < lo + 4, ro[1], ro[2]))

    def merge(w, e):
        return jnp.where(lax.rem(lane, 2) == 0, w * mw, pltpu.roll(e, 126, 1) * mx)

    def row_at(p):
        return pl.multiple_of(p * PH + 8, 8)

    def uedge(i, _):
        for side, row in ((0, 8), (1, 39)):
            ev[side, pl.ds(pl.multiple_of(i * 8, 8), 8), :] = ub[pl.ds(8 * i * PH + row, 8, stride=PH), :]
        return 0

    lax.fori_loop(0, 10, uedge, 0)
    pack_rows(0, 0)
    pack_rows(0, 1)

    def lane_of(l):
        i = l - 1
        return lax.div(i, 20), lax.rem(i, 20) * 6 + 2

    def edge_pair(k, p):
        for d in range(2):
            l = 2 * p + 1 + d
            tile, lo = lane_of(l)
            vals = [tb[pl.ds(row_at(l * 3 + v), 32), :] for v in range(3)]
            put(ec.at[k, tile], three(vals, lo), lo, 6)

    def cedge(p, _):
        edge_pair(0, p)
        return 0

    lax.fori_loop(0, 37, cedge, 0)

    def vlane(l):
        return lax.div(l, 60), lax.rem(l, 60) * 2 + 2

    def vedge(p, _):
        for d in range(3):
            tile, lo = vlane(3 * p + d)
            put(cv.at[tile], edge(u1[3 * p + d], lo), lo, 2)
        return 0

    lax.fori_loop(0, 25, vedge, 0)

    up = (lax.rem(A + 15, 16), O)
    down = (lax.rem(A + 1, 16), O)
    west = (A, lax.rem(O + 7, 8))
    east = (A, lax.rem(O + 1, 8))
    mk = pltpu.make_async_remote_copy

    def halo(k, g):
        rows = pl.ds(0, 8 * GROUPS[g][1])
        tiles = pl.ds(2 * g, 2)
        return [
            mk(er.at[k, g, 0, rows], hr.at[k, g, 1, rows], hs.at[k, g, 0], hrs.at[k, g, 0], device_id=up, device_id_type=MESH),
            mk(er.at[k, g, 1, rows], hr.at[k, g, 0, rows], hs.at[k, g, 1], hrs.at[k, g, 1], device_id=down, device_id_type=MESH),
            mk(ec.at[k, tiles], hc.at[k, 1, tiles], hs.at[k, g, 2], hrs.at[k, g, 2], device_id=west, device_id_type=MESH),
            mk(ec.at[k, tiles], hc.at[k, 0, tiles], hs.at[k, g, 3], hrs.at[k, g, 3], device_id=east, device_id_type=MESH),
        ]

    def halo0(k):
        return [
            mk(er0.at[k, 0], hr0.at[k, 1], hs0.at[k, 0], hr0s.at[k, 0], device_id=up, device_id_type=MESH),
            mk(er0.at[k, 1], hr0.at[k, 0], hs0.at[k, 1], hr0s.at[k, 1], device_id=down, device_id_type=MESH),
            mk(ec0.at[k], hc0.at[k, 1], hs0.at[k, 2], hr0s.at[k, 2], device_id=west, device_id_type=MESH),
            mk(ec0.at[k], hc0.at[k, 0], hs0.at[k, 3], hr0s.at[k, 3], device_id=east, device_id_type=MESH),
        ]

    pl.semaphore_wait(bar, NDEV - 1)
    H = [[halo(k, g) for g in range(2)] for k in range(4)]
    HV = [
        mk(ev.at[0], hv.at[1], hsv.at[0], hrv.at[0], device_id=up, device_id_type=MESH),
        mk(ev.at[1], hv.at[0], hsv.at[1], hrv.at[1], device_id=down, device_id_type=MESH),
        mk(cv, hcv.at[1], hsv.at[2], hrv.at[2], device_id=west, device_id_type=MESH),
        mk(cv, hcv.at[0], hsv.at[3], hrv.at[3], device_id=east, device_id_type=MESH),
    ]
    H0 = [halo0(k) for k in range(4)]

    def start(cs):
        for cp in cs:
            cp.start()

    def arrive(cs):
        for cp in cs:
            cp.wait_recv()

    def send_all(src, dst, ssem, rsem):
        to_all(lambda a, o: pltpu.make_async_remote_copy(
            src.at[a * 8 + o], dst.at[me], ssem, rsem, device_id=(a, o), device_id_type=MESH).start())

    def bulk(ref, sem):
        pltpu.make_async_copy(ref.at[pl.ds(0, NDEV - 1)], ref.at[pl.ds(0, NDEV - 1)], sem).wait()

    start(HV)
    start(H[0][0])
    start(H[0][1])
    send_all(sb_ref, arr, asem.at[0], asem.at[1])
    own = pltpu.make_async_copy(sb_ref.at[me], arr.at[me], asem.at[4])
    own.start()

    def tiles_in(k, g):
        for t in range(2 * g, 2 * g + 2):
            xc[t] = merge(hc[k, 0, t], hc[k, 1, t])

    def advance(l, xt, lo):
        co = [cb[pl.ds(pl.multiple_of((l * 5 + j) * 32, 8), 32), :] for j in range(5)]
        vals = []
        for v in range(3):
            base = (l * 3 + v) * PH
            t = tb[pl.ds(pl.multiple_of(base + 8, 8), 32), :]
            tn = tb[pl.ds(base + 7, 32), :]
            ts = tb[pl.ds(base + 9, 32), :]
            h = pltpu.roll(xt, 128 - (lo + 2 * v), 1)
            tw = jnp.where(lane == 0, h, pltpu.roll(t, 1, 1))
            te = jnp.where(lane == 127, h, pltpu.roll(t, 127, 1))
            vals.append(co[0] * t + co[1] * tn + co[2] * ts + co[3] * tw + co[4] * te)
        return vals

    def keep(l, vals):
        for v in range(3):
            tb[pl.ds(row_at(l * 3 + v), 32), :] = vals[v]

    def move_pair(p):
        out = []
        for d in range(2):
            l = 2 * p + 1 + d
            tile, lo = lane_of(l)
            out.append((l, advance(l, xc[tile], lo)))
        return out

    def keep_pair(out):
        for l, vals in out:
            keep(l, vals)

    def main_round(k, g):
        first, last = GROUPS[g][2:]
        keep_pair(move_pair(first))

        def f(p, _):
            out = move_pair(p)
            if k < 3:
                edge_pair(k + 1, p - 1)
            keep_pair(out)
            return 0

        lax.fori_loop(first + 1, last, f, 0)
        if k < 3:
            edge_pair(k + 1, last - 1)
            pack_rows(k + 1, g)
            start(H[k + 1][g])

    def coefs():
        xv = [merge(hcv[0, t], hcv[1, t]) for t in range(2)]
        xc[4] = xv[0]
        xc[5] = xv[1]

        def hrow(i, _):
            for side, row, m in ((0, 7, mn), (1, 40, ms)):
                ub[pl.ds(8 * i * PH + row, 8, stride=PH), :] = hv[side, pl.ds(pl.multiple_of(i * 8, 8), 8), :] * m
            return 0

        lax.fori_loop(0, 10, hrow, 0)

        def one(l):
            base = l * PH
            a = ub[pl.ds(pl.multiple_of(base + 8, 8), 32), :]
            fn = 0.5 * (ub[pl.ds(base + 7, 32), :] + a)
            fs = 0.5 * (a + ub[pl.ds(base + 9, 32), :])
            b = u1[l]
            tile, lo = vlane(l)
            h = pltpu.roll(xc[4 + tile], 128 - lo, 1)
            fw = 0.5 * (jnp.where(lane == 0, h, pltpu.roll(b, 1, 1)) + b)
            fe = 0.5 * (b + jnp.where(lane == 127, h, pltpu.roll(b, 127, 1)))
            zero = jnp.zeros_like(a)
            mid = 1.0 - jnp.maximum(fs, zero) + jnp.minimum(fn, zero) - jnp.maximum(fe, zero) + jnp.minimum(fw, zero)
            outs = (mid, jnp.maximum(fn, zero), -jnp.minimum(fs, zero), jnp.maximum(fw, zero), -jnp.minimum(fe, zero))
            return outs

        def f(p, _):
            outs = [one(3 * p + d) for d in range(3)]
            for d in range(3):
                for j in range(5):
                    cb[pl.ds(pl.multiple_of(((3 * p + d) * 5 + j) * 32, 8), 32), :] = outs[d][j]
            return 0

        lax.fori_loop(0, 25, f, 0)

    def step(k, g):
        arrive(H[k][g])
        unpack_rows(k, g)
        tiles_in(k, g)
        main_round(k, g)

    arrive(HV)
    coefs()
    for k in range(2):
        step(k, 0)
        step(k, 1)

    own.wait()
    bulk(arr, asem.at[1])
    summed = jnp.dot(sel[...], arr[...].reshape(2048, 128), preferred_element_type=F32)
    h = jnp.where(kind_ref[...] == 0, 0.0, hx_ref[...])
    den = 1.0 + h * summed[96:128]
    zb = jnp.zeros((32, 128), BF16)
    parts = []
    forced = []
    for v in range(3):
        t0 = tb[pl.ds(v * PH + 8, 32), :]
        surf = jnp.where(kind_ref[...] == 2, ice_ref[v], t0)
        flux = h * (surf - summed[32 * v:32 * v + 32]) / den
        parts.append(flux.astype(BF16))
        t0 = t0 - flux
        tb[pl.ds(v * PH + 8, 32), :] = t0
        forced.append(t0)
    fb = jnp.concatenate(parts + [zb], axis=0)
    ret = lax.dot_general(sel[...], fb, (((0,), (0,)), ((), ())), preferred_element_type=F32)
    rb[...] = ret.astype(BF16).reshape(NDEV, 16, 128)
    send_all(rb, ans_ref, asem.at[2], asem.at[3])
    own2 = pltpu.make_async_copy(rb.at[me], ans_ref.at[me], asem.at[5])
    own2.start()

    def send_zero(k, vals):
        for side, row in ((0, 8), (1, 39)):
            er0[k, side, :, :] = tb[pl.ds(row, 8, stride=PH), :]
        ec0[k] = three(vals, 2)
        start(H0[k])

    def recv_zero(k):
        arrive(H0[k])
        for side, row, m in ((0, 7, mn), (1, 40, ms)):
            tb[pl.ds(row, 3, stride=PH), :] = hr0[k, side, 0:3, :] * m
        vals = advance(0, merge(hc0[k, 0], hc0[k, 1]), 2)
        keep(0, vals)
        return vals

    send_zero(0, forced)
    step(2, 0)
    send_zero(1, recv_zero(0))
    step(2, 1)
    send_zero(2, recv_zero(1))
    step(3, 0)
    send_zero(3, recv_zero(2))
    step(3, 1)
    outs = [pltpu.make_async_copy(tb4.at[pl.ds(1, OL - 1), v, pl.ds(8, 32)], oc_hbm.at[v, pl.ds(1, OL - 1)], osem.at[v]) for v in range(3)]
    start(outs)
    recv_zero(3)
    outs0 = [pltpu.make_async_copy(tb4.at[0, v, pl.ds(8, 32)], oc_hbm.at[v, 0], osem.at[3 + v]) for v in range(3)]
    start(outs0)
    own2.wait()
    bulk(ans_ref, asem.at[3])
    bulk(sb_ref, asem.at[0])
    bulk(rb, asem.at[2])
    for cs in [c for pair in H for c in pair] + [HV] + H0:
        for cp in cs:
            cp.wait_send()
    for cp in outs + outs0:
        cp.wait()


def rk(sb, val, tracer, velocity, hx, kind, ice):
    D = pltpu.SemaphoreType.DMA
    V = pltpu.VMEM
    return pl.pallas_call(
        rk_body,
        out_shape=(jax.ShapeDtypeStruct((NDEV, 16, 128), BF16), jax.ShapeDtypeStruct((3, OL, 32, 128), F32)),
        in_specs=[VM, VM, ANY, ANY, ANY, ANY, ANY],
        out_specs=(VM, ANY),
        scratch_shapes=[
            V((32, 128), F32), V((32, 128), I32), V((3, 32, 128), F32), V((PLANES * PH, 128), F32), V((OL * 5 * 32, 128), F32), V((80 * PH, 128), F32), V((OL, 32, 128), F32),
            V((4, 2, 2, 120, 128), F32), V((4, 2, 2, 120, 128), F32), V((4, 4, 32, 128), F32), V((4, 2, 4, 32, 128), F32),
            V((2, 80, 128), F32), V((2, 80, 128), F32), V((2, 32, 128), F32), V((2, 2, 32, 128), F32), V((6, 32, 128), F32),
            V((4, 2, 8, 128), F32), V((4, 2, 8, 128), F32), V((4, 32, 128), F32), V((4, 2, 32, 128), F32),
            V((NDEV, 16, 128), BF16), V((NDEV, 16, 128), BF16), V((128, 2048), BF16),
            D((8,)), D((6,)), D((4, 2, 4)), D((4, 2, 4)), D((4,)), D((4,)), D((4, 4)), D((4, 4)), D((6,)),
        ],
        compiler_params=pltpu.CompilerParams(collective_id=0, has_side_effects=True, vmem_limit_bytes=62 << 20),
        name="exchange_ocean",
    )(sb, val, tracer, velocity, hx, kind, ice)

def per_device(atm_state, diffusivity, send_slot, atm_block, recv_row, remap_weight, ocean_tracer, ocean_velocity,
               exchange_coef, surface_kind, ice_surface):
    slot, ablk = send_slot[0], atm_block[0]
    sb, c, g, r = k1(slot, ablk, atm_state, diffusivity, remap_weight)
    lanes = jnp.arange(2048, dtype=I32)
    rr = jnp.repeat(recv_row[0], 4)
    val = jnp.where(rr >= 0, rr + 32 * (lanes % 4), -1)[None, :]
    ans, ocean = rk(sb.reshape(128, 16, 128), val, ocean_tracer, ocean_velocity, exchange_coef, surface_kind, ice_surface)
    return k3(slot, ablk, ans.reshape(2048, 128), remap_weight, c, g, r, ocean)


def solution(mesh):
    placed = (
        P(None, None, ("atm", "ocn")),
        P(None, ("atm", "ocn")),
        P(("atm", "ocn"), None),
        P(("atm", "ocn"), None),
        P(("atm", "ocn"), None),
        P(("atm", "ocn"), None, None),
        P(None, None, "atm", "ocn"),
        P(None, None, "atm", "ocn"),
        P("atm", "ocn"),
        P("atm", "ocn"),
        P(None, "atm", "ocn"),
    )
    return jax.shard_map(
        per_device,
        mesh=mesh,
        in_specs=placed,
        out_specs=(P(None, None, ("atm", "ocn")), P(None, None, "atm", "ocn")),
        check_vma=False,
    )
```

```python
import functools
import jax
import jax.numpy as jnp
from jax import lax
from jax.experimental import pallas as pl
from jax.experimental.pallas import tpu as pltpu
from jax.sharding import PartitionSpec as P

F32, BF16, I32 = jnp.float32, jnp.bfloat16, jnp.int32
MESH = pl.DeviceIdType.MESH
VM = pl.BlockSpec(memory_space=pltpu.VMEM)
SM = pl.BlockSpec(memory_space=pltpu.SMEM)
ANY = pl.BlockSpec(memory_space=pltpu.HBM)
NV, LEV, NBLK, AB, SLOTS = 3, 63, 256, 16, 512
WCH = 16


def w_copy(w_hbm, w_ref, sem, i):
    n = NBLK // WCH
    rows = pl.ds(i * n, n)
    return pltpu.make_async_copy(w_hbm.at[rows], w_ref.at[rows], sem.at[i])


def w_copies(w_hbm, w_ref, sem):
    return [w_copy(w_hbm, w_ref, sem, i) for i in range(WCH)]


def k1_body(slot_ref, ablk_ref, atm_hbm, dif_hbm, w_hbm, sb_ref, c_hbm, g_hbm, r_ref,
            w_ref, atm_ref, dif_ref, c_ref, g_ref, s_ref, d_ref, pk_ref, sl_ref, sem, isem):
    ins = [pltpu.make_async_copy(atm_hbm, atm_ref, isem.at[0]), pltpu.make_async_copy(dif_hbm, dif_ref, isem.at[1])]
    cps = w_copies(w_hbm, w_ref, sem)
    for cp in ins + cps:
        cp.start()
    sl_ref[...] = jnp.zeros_like(sl_ref)
    for cp in ins:
        cp.wait()
    for v in range(NV + 1):
        rows = LEV if v < NV else LEV - 1
        for i in range(8):
            n = min(8, rows - 8 * i)
            for j in range(16):
                src = atm_ref[v, pl.ds(8 * i, n), pl.ds(128 * j, 128)] if v < NV else dif_ref[pl.ds(8 * i, n), pl.ds(128 * j, 128)]
                if v < NV:
                    s_ref[pl.ds(v * 1024 + 8 * i * 16 + j, n, stride=16), :] = src
                else:
                    d_ref[pl.ds(8 * i * 16 + j, n, stride=16), :] = src

    def level(k, kprev, know, c, g):
        den = 1.0 + kprev + know + kprev * c
        r = 1.0 / den
        gn = []
        for v in range(NV):
            gv = (s_ref[pl.ds(v * 1024 + k * 16, 16), :] + kprev * g[v]) * r
            g_ref[v, pl.ds(k * 16, 16), :] = gv
            gn.append(gv)
        return r, gn

    z = jnp.zeros((16, 128), F32)

    def step(k, carry):
        kprev, c, g = carry
        know = d_ref[pl.ds(k * 16, 16), :]
        r, gn = level(k, kprev, know, c, g)
        cn = -know * r
        c_ref[pl.ds(k * 16, 16), :] = cn
        return know, cn, gn

    kprev, c, g = lax.fori_loop(0, LEV - 1, step, (z, z, [z, z, z]), unroll=2)
    r, g = level(LEV - 1, kprev, z, c, g)
    r_ref[...] = r
    for f in range(4):
        val = g[f] if f < 3 else r
        pk_ref[pl.ds(f, 16, stride=8), :] = val
        pk_ref[pl.ds(f + 4, 16, stride=8), :] = val
    outs = [pltpu.make_async_copy(c_ref, c_hbm, isem.at[2]), pltpu.make_async_copy(g_ref, g_hbm, isem.at[3])]
    for cp in outs:
        cp.start()
    low = lax.broadcasted_iota(I32, (8, 128), 0) < 4

    def chunk(i, _):
        w_copy(w_hbm, w_ref, sem, i).wait()
        b = i * 16
        ys = []
        for q in range(4):
            xs = []
            for h in range(2):
                m0 = ablk_ref[0, b + 4 * q + 2 * h]
                m1 = ablk_ref[0, b + 4 * q + 2 * h + 1]
                x0 = pk_ref[pl.ds(pl.multiple_of(m0 * 8, 8), 8), :]
                x1 = pk_ref[pl.ds(pl.multiple_of(m1 * 8, 8), 8), :]
                xs.append(jnp.where(low, x0, x1).astype(BF16))
            for h in range(2):
                w = w_ref[pl.ds(b + 4 * q + 2 * h, 2)].reshape(256, 128)
                ys.append(lax.dot_general(xs[h], w, (((1,), (1,)), ((), ())), preferred_element_type=F32))
        for j in range(8):
            t0 = slot_ref[0, b + 2 * j]
            t1 = slot_ref[0, b + 2 * j + 1]
            sl_ref[pl.ds(t0 * 4, 4), :] = ys[j][0:4, 0:128]
            sl_ref[pl.ds(t1 * 4, 4), :] = ys[j][4:8, 128:256]
        return 0

    lax.fori_loop(0, WCH, chunk, 0)
    sb_ref[...] = sl_ref[...].astype(BF16)
    for cp in outs:
        cp.wait()


def k1(slot, ablk, atm, dif, w):
    return pl.pallas_call(
        k1_body,
        out_shape=(jax.ShapeDtypeStruct((2048, 128), BF16),
                   jax.ShapeDtypeStruct((1024, 128), F32),
                   jax.ShapeDtypeStruct((NV, 1024, 128), F32),
                   jax.ShapeDtypeStruct((16, 128), F32)),
        in_specs=[SM, SM, ANY, ANY, ANY],
        out_specs=(VM, ANY, ANY, VM),
        scratch_shapes=[pltpu.VMEM((NBLK, 128, 128), BF16), pltpu.VMEM((NV, LEV, 2048), F32), pltpu.VMEM((LEV - 1, 2048), F32),
                        pltpu.VMEM((1024, 128), F32), pltpu.VMEM((NV, 1024, 128), F32),
                        pltpu.VMEM((NV * 1024, 128), F32), pltpu.VMEM((1024, 128), F32), pltpu.VMEM((128, 128), F32),
                        pltpu.VMEM((2048, 128), F32), pltpu.SemaphoreType.DMA((WCH,)), pltpu.SemaphoreType.DMA((4,))],
        compiler_params=pltpu.CompilerParams(vmem_limit_bytes=62 << 20), name="down_forward",
    )(slot, ablk, atm, dif, w)


def k3_body(slot_ref, ablk_ref, ans_ref, w_hbm, c_hbm, g_hbm, r_ref, oc_in, out_hbm, oc_out,
            w_ref, c_ref, g_ref, oc_ref, af_ref, acc_ref, x_ref, out_ref, sem, isem, osem):
    cps = w_copies(w_hbm, w_ref, sem)
    ins = [pltpu.make_async_copy(c_hbm, c_ref, isem.at[0]), pltpu.make_async_copy(g_hbm, g_ref, isem.at[1])]
    oin = pltpu.make_async_copy(oc_in, oc_ref, isem.at[2])
    oout = pltpu.make_async_copy(oc_ref, oc_out, isem.at[3])
    for cp in cps + ins:
        cp.start()
    oin.start()
    af_ref[...] = ans_ref[...].astype(F32)
    acc_ref[...] = jnp.zeros_like(acc_ref)
    zero = jnp.zeros((4, 128), F32)

    def chunk(i, _):
        w_copy(w_hbm, w_ref, sem, i).wait()
        b = i * 16
        ys = []
        for q in range(8):
            x0 = af_ref[pl.ds(pl.multiple_of(slot_ref[0, b + 2 * q] * 4, 4), 4), :]
            x1 = af_ref[pl.ds(pl.multiple_of(slot_ref[0, b + 2 * q + 1] * 4, 4), 4), :]
            top = jnp.concatenate([x0, zero], axis=0)
            bot = jnp.concatenate([zero, x1], axis=0)
            x = jnp.concatenate([top, bot], axis=1).astype(BF16)
            ys.append(jnp.dot(x, w_ref[pl.ds(b + 2 * q, 2)].reshape(256, 128), preferred_element_type=F32))
        for j in range(16):
            m = pl.multiple_of(ablk_ref[0, b + j] * 8, 8)
            e = j % 2
            acc_ref[j % 8, pl.ds(m, 4), :] = acc_ref[j % 8, pl.ds(m, 4), :] + ys[j // 2][4 * e:4 * e + 4]
        return 0

    lax.fori_loop(0, WCH, chunk, 0)
    tot = acc_ref[0]
    for j in range(1, 8):
        tot = tot + acc_ref[j]
    acc_ref[0] = tot
    for cp in ins:
        cp.wait()
    oin.wait()
    oout.start()
    r = r_ref[...]
    xs = []
    for v in range(NV):
        sf = acc_ref[0, pl.ds(v, 16, stride=8), :]
        x = g_ref[v, pl.ds((LEV - 1) * 16, 16), :] + r * sf
        x_ref[pl.ds(v * 1024 + (LEV - 1) * 16, 16), :] = x
        xs.append(x)

    def down(k, xs):
        c = c_ref[pl.ds(k * 16, 16), :]
        new = []
        for v in range(NV):
            x = g_ref[v, pl.ds(k * 16, 16), :] - c * xs[v]
            x_ref[pl.ds(v * 1024 + k * 16, 16), :] = x
            new.append(x)
        return new

    def rows_out(i, n):
        for v in range(NV):
            for j in range(16):
                out_ref[v, pl.ds(8 * i, n), pl.ds(128 * j, 128)] = x_ref[pl.ds(v * 1024 + 8 * i * 16 + j, n, stride=16), :]

    for k in range(LEV - 2, 55, -1):
        xs = down(k, xs)
    rows_out(7, 7)

    def group(q, xs):
        i = 6 - q
        for d in range(8):
            xs = down(8 * i + 7 - d, xs)
        rows_out(i, 8)
        return xs

    lax.fori_loop(0, 7, group, xs)
    res = pltpu.make_async_copy(out_ref, out_hbm, osem)
    res.start()
    oout.wait()
    res.wait()


def k3(slot, ablk, ans, w, c, g, r, ocean):
    V = pltpu.VMEM
    return pl.pallas_call(
        k3_body,
        out_shape=(jax.ShapeDtypeStruct((NV, LEV, 2048), F32), jax.ShapeDtypeStruct((3, 75, 32, 128), F32)),
        in_specs=[SM, SM, VM, ANY, ANY, ANY, VM, ANY],
        out_specs=(ANY, ANY),
        scratch_shapes=[V((NBLK, 128, 128), BF16), V((1024, 128), F32), V((NV, 1024, 128), F32), V((3, 75, 32, 128), F32),
                        V((2048, 128), F32), V((8, 128, 128), F32), V((NV * 1024, 128), F32), V((NV, LEV, 2048), F32),
                        pltpu.SemaphoreType.DMA((WCH,)), pltpu.SemaphoreType.DMA((4,)), pltpu.SemaphoreType.DMA],
        compiler_params=pltpu.CompilerParams(vmem_limit_bytes=62 << 20), name="backward_up",
    )(slot, ablk, ans, w, c, g, r, ocean)

NDEV, OL, PH = 128, 75, 48
PLANES = 231
GROUPS = ((3, 15, 0, 10), (123, 13, 10, 19))


def rk_body(sb_ref, val_ref, tr_hbm, ve_hbm, hx_hbm, kind_hbm, ice_hbm, ans_ref, oc_hbm,
            hx_ref, kind_ref, ice_ref, tb, cb, ub, u1, er, hr, ec, hc, ev, hv, cv, hcv, xc, er0, hr0, ec0, hc0, arr, rb, sel,
            lsem, osem, hs, hrs, hsv, hrv, hs0, hr0s, asem):
    A = lax.axis_index("atm")
    O = lax.axis_index("ocn")
    me = A * 8 + O

    loads = []
    tb4 = tb.reshape(PLANES // 3, 3, PH, 128)
    ub3 = ub.reshape(80, PH, 128)
    for v in range(3):
        loads.append(pltpu.make_async_copy(tr_hbm.at[v], tb4.at[pl.ds(0, OL), v, pl.ds(8, 32)], lsem.at[v]))
    loads.append(pltpu.make_async_copy(ve_hbm.at[0], ub3.at[pl.ds(0, OL), pl.ds(8, 32)], lsem.at[3]))
    loads.append(pltpu.make_async_copy(ve_hbm.at[1], u1, lsem.at[4]))
    for i, (a, b) in enumerate(((hx_hbm, hx_ref), (kind_hbm, kind_ref), (ice_hbm, ice_ref))):
        loads.append(pltpu.make_async_copy(a, b, lsem.at[5 + i]))
    for cp in loads:
        cp.start()

    bar = pltpu.get_barrier_semaphore()

    cols = [lax.rem(O + j, 8) for j in range(8)]

    def to_all(fn):
        for j in range(1, 8):
            fn(A, cols[j])

        def f(i, _):
            a = lax.rem(A + i, 16)
            for j in range(8):
                fn(a, cols[j])
            return 0

        lax.fori_loop(1, 16, f, 0)

    to_all(lambda a, o: pl.semaphore_signal(bar, inc=1, device_id=(a, o), device_id_type=MESH))

    lane = lax.broadcasted_iota(I32, (32, 128), 1)
    mn = jnp.where(A > 0, 1.0, 0.0).astype(F32)
    ms = jnp.where(A < 15, 1.0, 0.0).astype(F32)
    mw = jnp.where(O > 0, 1.0, 0.0).astype(F32)
    mx = jnp.where(O < 7, 1.0, 0.0).astype(F32)

    spread = jnp.where(lax.broadcasted_iota(I32, (128, 512), 1) // 4 == lax.broadcasted_iota(I32, (128, 512), 0), 1.0, 0.0).astype(BF16)
    field = lax.rem(lax.broadcasted_iota(I32, (8, 512), 1), 4).astype(F32) * 32.0
    target = lax.broadcasted_iota(I32, (128, 512), 0).astype(F32)
    for q in range(4):
        rows = jnp.broadcast_to(val_ref[:, pl.ds(128 * q, 128)].astype(F32), (8, 128)).astype(BF16)
        wide = jnp.dot(rows, spread, preferred_element_type=F32)
        wide = jnp.where(wide >= 0.0, wide + field, -1.0)[0:1]
        sel[:, pl.ds(512 * q, 512)] = jnp.where(wide == target, 1.0, 0.0).astype(BF16)
    tb[pl.ds(OL * 3 * PH, 6 * PH), :] = jnp.zeros((6 * PH, 128), F32)
    cb[pl.ds(OL * 5 * 32, 2 * 5 * 32), :] = jnp.zeros((2 * 5 * 32, 128), F32)
    ub[pl.ds(OL * PH, 5 * PH), :] = jnp.zeros((5 * PH, 128), F32)
    ec[...] = jnp.zeros_like(ec)
    cv[...] = jnp.zeros_like(cv)
    ec0[...] = jnp.zeros_like(ec0)
    for cp in loads:
        cp.wait()

    def pack_rows(k, g):
        p0, n = GROUPS[g][:2]

        def f(i, _):
            for side, row in ((0, 8), (1, 39)):
                er[k, g, side, pl.ds(pl.multiple_of(i * 8, 8), 8), :] = tb[pl.ds((p0 + 8 * i) * PH + row, 8, stride=PH), :]
            return 0
        lax.fori_loop(0, n, f, 0)

    def unpack_rows(k, g):
        p0, n = GROUPS[g][:2]

        def f(i, _):
            for side, row, m in ((0, 7, mn), (1, 40, ms)):
                tb[pl.ds((p0 + 8 * i) * PH + row, 8, stride=PH), :] = hr[k, g, side, pl.ds(pl.multiple_of(i * 8, 8), 8), :] * m
            return 0
        lax.fori_loop(0, n, f, 0)

    couple = lax.rem(lane + 1, 128) // 2
    even = lax.rem(lane, 2) == 0

    def turn_of(l):
        return lax.rem(l, 64)

    def turned(x, l):
        return pltpu.roll(x, 2 * turn_of(l), 1)

    def straight(x, l):
        return pltpu.roll(x, lax.rem(128 - 2 * turn_of(l), 128), 1)

    def put(ref_view, val, l):
        pltpu.store(ref_view, val, mask=couple == turn_of(l))

    def merge(w, e):
        return jnp.where(even, pltpu.roll(w, 1, 1) * mw, pltpu.roll(e, 127, 1) * mx)

    def sides(x, h, l):
        here = couple == turn_of(l)
        tw = jnp.where(here & even, h, pltpu.roll(x, 1, 1))
        te = jnp.where(here & ~even, h, pltpu.roll(x, 127, 1))
        return tw, te

    def row_at(p):
        return pl.multiple_of(p * PH + 8, 8)

    def first_turn(g):
        def f(q, _):
            for d in range(4):
                l = 4 * q + 1 + d
                for v in range(3):
                    x = turned(tb[pl.ds(row_at(l * 3 + v), 32), :], l)
                    tb[pl.ds(row_at(l * 3 + v), 32), :] = x
                    put(ec.at[0, g, v], x, l)
            return 0
        lax.fori_loop(GROUPS[g][2], GROUPS[g][3], f, 0)
        pack_rows(0, g)

    def vturn(p, _):
        for d in range(5):
            l = 5 * p + d
            x = turned(u1[l], l)
            u1[l] = x
            put(cv.at[lax.div(l, 64)], x, l)
            row = pl.ds(pl.multiple_of(l * PH + 8, 8), 32)
            ub[row, :] = turned(ub[row, :], l)
        return 0

    lax.fori_loop(0, 15, vturn, 0)

    def uedge(i, _):
        for side, row in ((0, 8), (1, 39)):
            ev[side, pl.ds(pl.multiple_of(i * 8, 8), 8), :] = ub[pl.ds(8 * i * PH + row, 8, stride=PH), :]
        return 0

    lax.fori_loop(0, 10, uedge, 0)
    first_turn(0)
    first_turn(1)

    up = (lax.rem(A + 15, 16), O)
    down = (lax.rem(A + 1, 16), O)
    west = (A, lax.rem(O + 7, 8))
    east = (A, lax.rem(O + 1, 8))
    mk = pltpu.make_async_remote_copy

    def halo(k, g):
        rows = pl.ds(0, 8 * GROUPS[g][1])
        return [
            mk(er.at[k, g, 0, rows], hr.at[k, g, 1, rows], hs.at[k, g, 0], hrs.at[k, g, 0], device_id=up, device_id_type=MESH),
            mk(er.at[k, g, 1, rows], hr.at[k, g, 0, rows], hs.at[k, g, 1], hrs.at[k, g, 1], device_id=down, device_id_type=MESH),
            mk(ec.at[k, g], hc.at[k, g, 1], hs.at[k, g, 2], hrs.at[k, g, 2], device_id=west, device_id_type=MESH),
            mk(ec.at[k, g], hc.at[k, g, 0], hs.at[k, g, 3], hrs.at[k, g, 3], device_id=east, device_id_type=MESH),
        ]

    def halo0(k):
        return [
            mk(er0.at[k, 0], hr0.at[k, 1], hs0.at[k, 0], hr0s.at[k, 0], device_id=up, device_id_type=MESH),
            mk(er0.at[k, 1], hr0.at[k, 0], hs0.at[k, 1], hr0s.at[k, 1], device_id=down, device_id_type=MESH),
            mk(ec0.at[k], hc0.at[k, 1], hs0.at[k, 2], hr0s.at[k, 2], device_id=west, device_id_type=MESH),
            mk(ec0.at[k], hc0.at[k, 0], hs0.at[k, 3], hr0s.at[k, 3], device_id=east, device_id_type=MESH),
        ]

    pl.semaphore_wait(bar, NDEV - 1)
    H = [[halo(k, g) for g in range(2)] for k in range(4)]
    HV = [
        mk(ev.at[0], hv.at[1], hsv.at[0], hrv.at[0], device_id=up, device_id_type=MESH),
        mk(ev.at[1], hv.at[0], hsv.at[1], hrv.at[1], device_id=down, device_id_type=MESH),
        mk(cv, hcv.at[1], hsv.at[2], hrv.at[2], device_id=west, device_id_type=MESH),
        mk(cv, hcv.at[0], hsv.at[3], hrv.at[3], device_id=east, device_id_type=MESH),
    ]
    H0 = [halo0(k) for k in range(4)]

    def start(cs):
        for cp in cs:
            cp.start()

    def arrive(cs):
        for cp in cs:
            cp.wait_recv()

    def send_all(src, dst, ssem, rsem):
        to_all(lambda a, o: pltpu.make_async_remote_copy(
            src.at[a * 8 + o], dst.at[me], ssem, rsem, device_id=(a, o), device_id_type=MESH).start())

    def bulk(ref, sem):
        pltpu.make_async_copy(ref.at[pl.ds(0, NDEV - 1)], ref.at[pl.ds(0, NDEV - 1)], sem).wait()

    start(HV)
    start(H[0][0])
    start(H[0][1])
    send_all(sb_ref, arr, asem.at[0], asem.at[1])
    own = pltpu.make_async_copy(sb_ref.at[me], arr.at[me], asem.at[4])
    own.start()

    def tiles_in(k, g):
        for v in range(3):
            xc[g, v] = merge(hc[k, g, 0, v], hc[k, g, 1, v])

    def coef(l, j):
        return cb[pl.ds(pl.multiple_of((l * 5 + j) * 32, 8), 32), :]

    def advance(l, halo):
        ca, cn, cs, cw, ce = [coef(l, j) for j in range(5)]
        vals = []
        for v in range(3):
            base = (l * 3 + v) * PH
            t = tb[pl.ds(pl.multiple_of(base + 8, 8), 32), :]
            tn = tb[pl.ds(base + 7, 32), :]
            ts = tb[pl.ds(base + 9, 32), :]
            tw, te = sides(t, halo[v], l)
            vals.append(ca * t + cn * tn + cs * ts + cw * tw + ce * te)
        return vals

    def keep(l, vals):
        for v in range(3):
            tb[pl.ds(row_at(l * 3 + v), 32), :] = vals[v]

    def main_round(k, g):
        first, last = GROUPS[g][2:]

        def f(q, _):
            halo = [xc[g, v] for v in range(3)]
            for d in range(4):
                l = 4 * q + 1 + d
                vals = advance(l, halo)
                if k < 3:
                    for v in range(3):
                        put(ec.at[k + 1, g, v], vals[v], l)
                else:
                    vals = [straight(x, l) for x in vals]
                keep(l, vals)
            return 0

        lax.fori_loop(first, last, f, 0)
        if k < 3:
            pack_rows(k + 1, g)
            start(H[k + 1][g])

    def coefs():
        xv = [merge(hcv[0, t], hcv[1, t]) for t in range(2)]
        xc[2, 0] = xv[0]
        xc[2, 1] = xv[1]

        def hrow(i, _):
            for side, row, m in ((0, 7, mn), (1, 40, ms)):
                ub[pl.ds(8 * i * PH + row, 8, stride=PH), :] = hv[side, pl.ds(pl.multiple_of(i * 8, 8), 8), :] * m
            return 0

        lax.fori_loop(0, 10, hrow, 0)

        def one(l):
            base = l * PH
            a = ub[pl.ds(pl.multiple_of(base + 8, 8), 32), :]
            fn = 0.5 * (ub[pl.ds(base + 7, 32), :] + a)
            fs = 0.5 * (a + ub[pl.ds(base + 9, 32), :])
            b = u1[l]
            bw, be = sides(b, xc[2, lax.div(l, 64)], l)
            fw = 0.5 * (bw + b)
            fe = 0.5 * (b + be)
            zero = jnp.zeros_like(a)
            mid = 1.0 - jnp.maximum(fs, zero) + jnp.minimum(fn, zero) - jnp.maximum(fe, zero) + jnp.minimum(fw, zero)
            outs = (mid, jnp.maximum(fn, zero), -jnp.minimum(fs, zero), jnp.maximum(fw, zero), -jnp.minimum(fe, zero))
            return outs

        def f(p, _):
            outs = [one(5 * p + d) for d in range(5)]
            for d in range(5):
                for j in range(5):
                    cb[pl.ds(pl.multiple_of(((5 * p + d) * 5 + j) * 32, 8), 32), :] = outs[d][j]
            return 0

        lax.fori_loop(0, 15, f, 0)

    def step(k, g):
        arrive(H[k][g])
        unpack_rows(k, g)
        tiles_in(k, g)
        main_round(k, g)

    arrive(HV)
    coefs()
    for k in range(2):
        step(k, 0)
        step(k, 1)

    own.wait()
    bulk(arr, asem.at[1])
    summed = jnp.dot(sel[...], arr[...].reshape(2048, 128), preferred_element_type=F32)
    h = jnp.where(kind_ref[...] == 0, 0.0, hx_ref[...])
    den = 1.0 + h * summed[96:128]
    zb = jnp.zeros((32, 128), BF16)
    parts = []
    forced = []
    for v in range(3):
        t0 = tb[pl.ds(v * PH + 8, 32), :]
        surf = jnp.where(kind_ref[...] == 2, ice_ref[v], t0)
        flux = h * (surf - summed[32 * v:32 * v + 32]) / den
        parts.append(flux.astype(BF16))
        t0 = t0 - flux
        tb[pl.ds(v * PH + 8, 32), :] = t0
        forced.append(t0)
    fb = jnp.concatenate(parts + [zb], axis=0)
    ret = lax.dot_general(sel[...], fb, (((0,), (0,)), ((), ())), preferred_element_type=F32)
    rb[...] = ret.astype(BF16).reshape(NDEV, 16, 128)
    send_all(rb, ans_ref, asem.at[2], asem.at[3])
    own2 = pltpu.make_async_copy(rb.at[me], ans_ref.at[me], asem.at[5])
    own2.start()

    def send_zero(k, vals):
        for side, row in ((0, 8), (1, 39)):
            er0[k, side, :, :] = tb[pl.ds(row, 8, stride=PH), :]
        for v in range(3):
            ec0[k, v] = vals[v]
        start(H0[k])

    def recv_zero(k):
        arrive(H0[k])
        for side, row, m in ((0, 7, mn), (1, 40, ms)):
            tb[pl.ds(row, 3, stride=PH), :] = hr0[k, side, 0:3, :] * m
        vals = advance(0, [merge(hc0[k, 0, v], hc0[k, 1, v]) for v in range(3)])
        keep(0, vals)
        return vals

    def put_out(l0, l1, j):
        cs = [pltpu.make_async_copy(tb4.at[pl.ds(l0, l1 - l0), v, pl.ds(8, 32)], oc_hbm.at[v, pl.ds(l0, l1 - l0)], osem.at[j + v]) for v in range(3)]
        start(cs)
        return cs

    send_zero(0, forced)
    step(2, 0)
    send_zero(1, recv_zero(0))
    step(2, 1)
    send_zero(2, recv_zero(1))
    step(3, 0)
    outs = put_out(1, 41, 0)
    send_zero(3, recv_zero(2))
    step(3, 1)
    outs = outs + put_out(41, OL, 3)
    recv_zero(3)
    outs = outs + put_out(0, 1, 6)
    own2.wait()
    bulk(ans_ref, asem.at[3])
    bulk(sb_ref, asem.at[0])
    bulk(rb, asem.at[2])
    for cs in [c for pair in H for c in pair] + [HV] + H0:
        for cp in cs:
            cp.wait_send()
    for cp in outs:
        cp.wait()


def rk(sb, val, tracer, velocity, hx, kind, ice):
    D = pltpu.SemaphoreType.DMA
    V = pltpu.VMEM
    return pl.pallas_call(
        rk_body,
        out_shape=(jax.ShapeDtypeStruct((NDEV, 16, 128), BF16), jax.ShapeDtypeStruct((3, OL, 32, 128), F32)),
        in_specs=[VM, VM, ANY, ANY, ANY, ANY, ANY],
        out_specs=(VM, ANY),
        scratch_shapes=[
            V((32, 128), F32), V((32, 128), I32), V((3, 32, 128), F32), V((PLANES * PH, 128), F32), V((77 * 5 * 32, 128), F32), V((80 * PH, 128), F32), V((OL, 32, 128), F32),
            V((4, 2, 2, 120, 128), F32), V((4, 2, 2, 120, 128), F32), V((4, 2, 3, 32, 128), F32), V((4, 2, 2, 3, 32, 128), F32),
            V((2, 80, 128), F32), V((2, 80, 128), F32), V((2, 32, 128), F32), V((2, 2, 32, 128), F32), V((3, 3, 32, 128), F32),
            V((4, 2, 8, 128), F32), V((4, 2, 8, 128), F32), V((4, 3, 32, 128), F32), V((4, 2, 3, 32, 128), F32),
            V((NDEV, 16, 128), BF16), V((NDEV, 16, 128), BF16), V((128, 2048), BF16),
            D((8,)), D((9,)), D((4, 2, 4)), D((4, 2, 4)), D((4,)), D((4,)), D((4, 4)), D((4, 4)), D((6,)),
        ],
        compiler_params=pltpu.CompilerParams(collective_id=0, has_side_effects=True, vmem_limit_bytes=62 << 20),
        name="exchange_ocean",
    )(sb, val, tracer, velocity, hx, kind, ice)

def per_device(atm_state, diffusivity, send_slot, atm_block, recv_row, remap_weight, ocean_tracer, ocean_velocity,
               exchange_coef, surface_kind, ice_surface):
    sb, c, g, r = k1(send_slot, atm_block, atm_state, diffusivity, remap_weight)
    ans, ocean = rk(sb.reshape(128, 16, 128), recv_row, ocean_tracer, ocean_velocity, exchange_coef, surface_kind, ice_surface)
    return k3(send_slot, atm_block, ans.reshape(2048, 128), remap_weight, c, g, r, ocean)


def solution(mesh):
    placed = (
        P(None, None, ("atm", "ocn")),
        P(None, ("atm", "ocn")),
        P(("atm", "ocn"), None),
        P(("atm", "ocn"), None),
        P(("atm", "ocn"), None),
        P(("atm", "ocn"), None, None),
        P(None, None, "atm", "ocn"),
        P(None, None, "atm", "ocn"),
        P("atm", "ocn"),
        P("atm", "ocn"),
        P(None, "atm", "ocn"),
    )
    return jax.shard_map(
        per_device,
        mesh=mesh,
        in_specs=placed,
        out_specs=(P(None, None, ("atm", "ocn")), P(None, None, "atm", "ocn")),
        check_vma=False,
    )
```

```python
import functools
import jax
import jax.numpy as jnp
from jax import lax
from jax.experimental import pallas as pl
from jax.experimental.pallas import tpu as pltpu
from jax.sharding import PartitionSpec as P

F32, BF16, I32 = jnp.float32, jnp.bfloat16, jnp.int32
MESH = pl.DeviceIdType.MESH
VM = pl.BlockSpec(memory_space=pltpu.VMEM)
SM = pl.BlockSpec(memory_space=pltpu.SMEM)
ANY = pl.BlockSpec(memory_space=pltpu.HBM)
NV, LEV, NBLK, AB, SLOTS = 3, 63, 256, 16, 512
WCH = 16


def w_copy(w_hbm, w_ref, sem, i):
    n = NBLK // WCH
    rows = pl.ds(i * n, n)
    return pltpu.make_async_copy(w_hbm.at[rows], w_ref.at[rows], sem.at[i])


def w_copies(w_hbm, w_ref, sem):
    return [w_copy(w_hbm, w_ref, sem, i) for i in range(WCH)]


def k3_body(slot_ref, ablk_ref, ans_ref, w_hbm, c_hbm, g_hbm, r_ref, oc_in, out_hbm, oc_out,
            w_ref, c_ref, g_ref, oc_ref, af_ref, acc_ref, x_ref, out_ref, sem, isem, osem):
    cps = w_copies(w_hbm, w_ref, sem)
    ins = [pltpu.make_async_copy(c_hbm, c_ref, isem.at[0]), pltpu.make_async_copy(g_hbm, g_ref, isem.at[1])]
    oin = pltpu.make_async_copy(oc_in, oc_ref, isem.at[2])
    oout = pltpu.make_async_copy(oc_ref, oc_out, isem.at[3])
    for cp in cps + ins:
        cp.start()
    oin.start()
    af_ref[...] = ans_ref[...].astype(F32)
    acc_ref[...] = jnp.zeros_like(acc_ref)
    zero = jnp.zeros((4, 128), F32)

    def chunk(i, _):
        w_copy(w_hbm, w_ref, sem, i).wait()
        b = i * 16
        ys = []
        for q in range(8):
            x0 = af_ref[pl.ds(pl.multiple_of(slot_ref[0, b + 2 * q] * 4, 4), 4), :]
            x1 = af_ref[pl.ds(pl.multiple_of(slot_ref[0, b + 2 * q + 1] * 4, 4), 4), :]
            top = jnp.concatenate([x0, zero], axis=0)
            bot = jnp.concatenate([zero, x1], axis=0)
            x = jnp.concatenate([top, bot], axis=1).astype(BF16)
            ys.append(jnp.dot(x, w_ref[pl.ds(b + 2 * q, 2)].reshape(256, 128), preferred_element_type=F32))
        for j in range(16):
            m = pl.multiple_of(ablk_ref[0, b + j] * 8, 8)
            e = j % 2
            acc_ref[j % 8, pl.ds(m, 4), :] = acc_ref[j % 8, pl.ds(m, 4), :] + ys[j // 2][4 * e:4 * e + 4]
        return 0

    lax.fori_loop(0, WCH, chunk, 0)
    tot = acc_ref[0]
    for j in range(1, 8):
        tot = tot + acc_ref[j]
    acc_ref[0] = tot
    for cp in ins:
        cp.wait()
    oin.wait()
    oout.start()
    r = r_ref[...]
    xs = []
    for v in range(NV):
        sf = acc_ref[0, pl.ds(v, 16, stride=8), :]
        x = g_ref[v, pl.ds((LEV - 1) * 16, 16), :] + r * sf
        x_ref[pl.ds(v * 1024 + (LEV - 1) * 16, 16), :] = x
        xs.append(x)

    def down(k, xs):
        c = c_ref[pl.ds(k * 16, 16), :]
        new = []
        for v in range(NV):
            x = g_ref[v, pl.ds(k * 16, 16), :] - c * xs[v]
            x_ref[pl.ds(v * 1024 + k * 16, 16), :] = x
            new.append(x)
        return new

    def rows_out(i, n):
        for v in range(NV):
            for j in range(16):
                out_ref[v, pl.ds(8 * i, n), pl.ds(128 * j, 128)] = x_ref[pl.ds(v * 1024 + 8 * i * 16 + j, n, stride=16), :]

    for k in range(LEV - 2, 55, -1):
        xs = down(k, xs)
    rows_out(7, 7)

    def group(q, xs):
        i = 6 - q
        for d in range(8):
            xs = down(8 * i + 7 - d, xs)
        rows_out(i, 8)
        return xs

    lax.fori_loop(0, 7, group, xs)
    res = pltpu.make_async_copy(out_ref, out_hbm, osem)
    res.start()
    oout.wait()
    res.wait()


def k3(slot, ablk, ans, w, c, g, r, ocean):
    V = pltpu.VMEM
    return pl.pallas_call(
        k3_body,
        out_shape=(jax.ShapeDtypeStruct((NV, LEV, 2048), F32), jax.ShapeDtypeStruct((3, 75, 32, 128), F32)),
        in_specs=[SM, SM, VM, ANY, ANY, ANY, VM, ANY],
        out_specs=(ANY, ANY),
        scratch_shapes=[V((NBLK, 128, 128), BF16), V((1024, 128), F32), V((NV, 1024, 128), F32), V((3, 75, 32, 128), F32),
                        V((2048, 128), F32), V((8, 128, 128), F32), V((NV * 1024, 128), F32), V((NV, LEV, 2048), F32),
                        pltpu.SemaphoreType.DMA((WCH,)), pltpu.SemaphoreType.DMA((4,)), pltpu.SemaphoreType.DMA],
        compiler_params=pltpu.CompilerParams(vmem_limit_bytes=62 << 20), name="backward_up",
    )(slot, ablk, ans, w, c, g, r, ocean)

NDEV, OL, PH = 128, 75, 48
PLANES = 231
GROUPS = ((3, 15, 0, 10), (123, 13, 10, 19))


def rk_body(ablk_row, slot_row, val_ref, atm_hbm, dif_hbm, w_hbm, tr_hbm, ve_hbm, hx_hbm, kind_hbm, ice_hbm,
            ans_ref, oc_hbm, c_hbm, g_hbm, r_ref,
            w_ref, atm_ref, dif_ref, c_ref, g_ref, s_ref, d_ref, pk_ref, cf_ref, sl_ref, sb_ref, wsem, isem,
            hx_ref, kind_ref, ice_ref, tb, cb, ub, u1, er, hr, ec, hc, ev, hv, cv, hcv, xc, er0, hr0, ec0, hc0, arr, rb, sel,
            lsem, osem, hs, hrs, hsv, hrv, hs0, hr0s, asem):
    A = lax.axis_index("atm")
    O = lax.axis_index("ocn")
    me = A * 8 + O

    ins = [pltpu.make_async_copy(atm_hbm, atm_ref, isem.at[0]), pltpu.make_async_copy(dif_hbm, dif_ref, isem.at[1])]
    for cp in ins:
        cp.start()
    loads = []
    tb4 = tb.reshape(PLANES // 3, 3, PH, 128)
    ub3 = ub.reshape(80, PH, 128)
    for v in range(3):
        loads.append(pltpu.make_async_copy(tr_hbm.at[v], tb4.at[pl.ds(0, OL), v, pl.ds(8, 32)], lsem.at[v]))
    loads.append(pltpu.make_async_copy(ve_hbm.at[0], ub3.at[pl.ds(0, OL), pl.ds(8, 32)], lsem.at[3]))
    loads.append(pltpu.make_async_copy(ve_hbm.at[1], u1, lsem.at[4]))
    for i, (a, b) in enumerate(((hx_hbm, hx_ref), (kind_hbm, kind_ref), (ice_hbm, ice_ref))):
        loads.append(pltpu.make_async_copy(a, b, lsem.at[5 + i]))
    loads = loads[3:5] + loads[:3] + loads[5:]
    for cp in loads + w_copies(w_hbm, w_ref, wsem):
        cp.start()

    bar = pltpu.get_barrier_semaphore()

    cols = [lax.rem(O + j, 8) for j in range(8)]

    def to_all(fn):
        for j in range(1, 8):
            fn(A, cols[j])

        def f(i, _):
            a = lax.rem(A + i, 16)
            for j in range(8):
                fn(a, cols[j])
            return 0

        lax.fori_loop(1, 16, f, 0)

    to_all(lambda a, o: pl.semaphore_signal(bar, inc=1, device_id=(a, o), device_id_type=MESH))

    lane = lax.broadcasted_iota(I32, (32, 128), 1)
    mn = jnp.where(A > 0, 1.0, 0.0).astype(F32)
    ms = jnp.where(A < 15, 1.0, 0.0).astype(F32)
    mw = jnp.where(O > 0, 1.0, 0.0).astype(F32)
    mx = jnp.where(O < 7, 1.0, 0.0).astype(F32)

    for cp in ins:
        cp.wait()
    for v in range(NV + 1):
        rows = LEV if v < NV else LEV - 1
        for i in range(8):
            n = min(8, rows - 8 * i)
            for j in range(16):
                src = atm_ref[v, pl.ds(8 * i, n), pl.ds(128 * j, 128)] if v < NV else dif_ref[pl.ds(8 * i, n), pl.ds(128 * j, 128)]
                if v < NV:
                    s_ref[pl.ds(v * 1024 + 8 * i * 16 + j, n, stride=16), :] = src
                else:
                    d_ref[pl.ds(8 * i * 16 + j, n, stride=16), :] = src

    def level(k, kprev, know, c, g):
        den = 1.0 + kprev + know + kprev * c
        r = 1.0 / den
        gn = []
        for v in range(NV):
            gv = (s_ref[pl.ds(v * 1024 + k * 16, 16), :] + kprev * g[v]) * r
            g_ref[v, pl.ds(k * 16, 16), :] = gv
            gn.append(gv)
        return r, gn

    z = jnp.zeros((16, 128), F32)

    def step(k, carry):
        kprev, c, g = carry
        know = d_ref[pl.ds(k * 16, 16), :]
        r, gn = level(k, kprev, know, c, g)
        cn = -know * r
        c_ref[pl.ds(k * 16, 16), :] = cn
        return know, cn, gn

    kprev, c, g = lax.fori_loop(0, LEV - 1, step, (z, z, [z, z, z]), unroll=2)
    r, g = level(LEV - 1, kprev, z, c, g)
    r_ref[...] = r
    for f in range(4):
        val = g[f] if f < 3 else r
        pk_ref[pl.ds(f, 16, stride=4), :] = val
    cg = [pltpu.make_async_copy(c_ref, c_hbm, isem.at[2]), pltpu.make_async_copy(g_ref, g_hbm, isem.at[3])]
    for cp in cg:
        cp.start()

    spread = jnp.where(lax.broadcasted_iota(I32, (128, 512), 1) // 4 == lax.broadcasted_iota(I32, (128, 512), 0), 1.0, 0.0).astype(BF16)
    field = lax.rem(lax.broadcasted_iota(I32, (8, 512), 1), 4).astype(F32) * 32.0
    target = lax.broadcasted_iota(I32, (128, 512), 0).astype(F32)


    def widen(ref, q):
        rows = jnp.broadcast_to(ref[:, pl.ds(128 * q, 128)].astype(F32), (8, 128)).astype(BF16)
        return jnp.dot(rows, spread, preferred_element_type=F32)

    for q in range(4):
        wide = widen(val_ref, q)
        wide = jnp.where(wide >= 0.0, wide + field, -1.0)[0:1]
        sel[:, pl.ds(512 * q, 512)] = jnp.where(wide == target, 1.0, 0.0).astype(BF16)
    tb[pl.ds(OL * 3 * PH, 6 * PH), :] = jnp.zeros((6 * PH, 128), F32)
    cb[pl.ds(OL * 5 * 32, 2 * 5 * 32), :] = jnp.zeros((2 * 5 * 32, 128), F32)
    ub[pl.ds(OL * PH, 5 * PH), :] = jnp.zeros((5 * PH, 128), F32)
    ec[...] = jnp.zeros_like(ec)
    cv[...] = jnp.zeros_like(cv)
    ec0[...] = jnp.zeros_like(ec0)
    for cp in loads:
        cp.wait()

    def pack_rows(k, g):
        p0, n = GROUPS[g][:2]

        def f(i, _):
            for side, row in ((0, 8), (1, 39)):
                er[k, g, side, pl.ds(pl.multiple_of(i * 8, 8), 8), :] = tb[pl.ds((p0 + 8 * i) * PH + row, 8, stride=PH), :]
            return 0
        lax.fori_loop(0, n, f, 0)

    def unpack_rows(k, g):
        p0, n = GROUPS[g][:2]

        def f(i, _):
            for side, row, m in ((0, 7, mn), (1, 40, ms)):
                tb[pl.ds((p0 + 8 * i) * PH + row, 8, stride=PH), :] = hr[k, g, side, pl.ds(pl.multiple_of(i * 8, 8), 8), :] * m
            return 0
        lax.fori_loop(0, n, f, 0)

    couple = lax.rem(lane + 1, 128) // 2
    even = lax.rem(lane, 2) == 0

    def turn_of(l):
        return lax.rem(l, 64)

    def turned(x, l):
        return pltpu.roll(x, 2 * turn_of(l), 1)

    def straight(x, l):
        return pltpu.roll(x, lax.rem(128 - 2 * turn_of(l), 128), 1)

    def put(ref_view, val, l):
        pltpu.store(ref_view, val, mask=couple == turn_of(l))

    def merge(w, e):
        return jnp.where(even, pltpu.roll(w, 1, 1) * mw, pltpu.roll(e, 127, 1) * mx)

    def sides(x, h, l):
        here = couple == turn_of(l)
        tw = jnp.where(here & even, h, pltpu.roll(x, 1, 1))
        te = jnp.where(here & ~even, h, pltpu.roll(x, 127, 1))
        return tw, te

    def row_at(p):
        return pl.multiple_of(p * PH + 8, 8)

    def first_turn(g):
        def f(q, _):
            for d in range(4):
                l = 4 * q + 1 + d
                for v in range(3):
                    x = turned(tb[pl.ds(row_at(l * 3 + v), 32), :], l)
                    tb[pl.ds(row_at(l * 3 + v), 32), :] = x
                    put(ec.at[0, g, v], x, l)
            return 0
        lax.fori_loop(GROUPS[g][2], GROUPS[g][3], f, 0)
        pack_rows(0, g)

    def vturn(p, _):
        for d in range(5):
            l = 5 * p + d
            x = turned(u1[l], l)
            u1[l] = x
            put(cv.at[lax.div(l, 64)], x, l)
            row = pl.ds(pl.multiple_of(l * PH + 8, 8), 32)
            ub[row, :] = turned(ub[row, :], l)
        return 0

    lax.fori_loop(0, 15, vturn, 0)

    def uedge(i, _):
        for side, row in ((0, 8), (1, 39)):
            ev[side, pl.ds(pl.multiple_of(i * 8, 8), 8), :] = ub[pl.ds(8 * i * PH + row, 8, stride=PH), :]
        return 0

    lax.fori_loop(0, 10, uedge, 0)
    first_turn(0)
    first_turn(1)

    up = (lax.rem(A + 15, 16), O)
    down = (lax.rem(A + 1, 16), O)
    west = (A, lax.rem(O + 7, 8))
    east = (A, lax.rem(O + 1, 8))
    mk = pltpu.make_async_remote_copy

    def halo(k, g):
        rows = pl.ds(0, 8 * GROUPS[g][1])
        return [
            mk(er.at[k, g, 0, rows], hr.at[k, g, 1, rows], hs.at[k, g, 0], hrs.at[k, g, 0], device_id=up, device_id_type=MESH),
            mk(er.at[k, g, 1, rows], hr.at[k, g, 0, rows], hs.at[k, g, 1], hrs.at[k, g, 1], device_id=down, device_id_type=MESH),
            mk(ec.at[k, g], hc.at[k, g, 1], hs.at[k, g, 2], hrs.at[k, g, 2], device_id=west, device_id_type=MESH),
            mk(ec.at[k, g], hc.at[k, g, 0], hs.at[k, g, 3], hrs.at[k, g, 3], device_id=east, device_id_type=MESH),
        ]

    def halo0(k):
        return [
            mk(er0.at[k, 0], hr0.at[k, 1], hs0.at[k, 0], hr0s.at[k, 0], device_id=up, device_id_type=MESH),
            mk(er0.at[k, 1], hr0.at[k, 0], hs0.at[k, 1], hr0s.at[k, 1], device_id=down, device_id_type=MESH),
            mk(ec0.at[k], hc0.at[k, 1], hs0.at[k, 2], hr0s.at[k, 2], device_id=west, device_id_type=MESH),
            mk(ec0.at[k], hc0.at[k, 0], hs0.at[k, 3], hr0s.at[k, 3], device_id=east, device_id_type=MESH),
        ]

    pl.semaphore_wait(bar, NDEV - 1)
    H = [[halo(k, g) for g in range(2)] for k in range(4)]
    HV = [
        mk(ev.at[0], hv.at[1], hsv.at[0], hrv.at[0], device_id=up, device_id_type=MESH),
        mk(ev.at[1], hv.at[0], hsv.at[1], hrv.at[1], device_id=down, device_id_type=MESH),
        mk(cv, hcv.at[1], hsv.at[2], hrv.at[2], device_id=west, device_id_type=MESH),
        mk(cv, hcv.at[0], hsv.at[3], hrv.at[3], device_id=east, device_id_type=MESH),
    ]
    H0 = [halo0(k) for k in range(4)]

    def start(cs):
        for cp in cs:
            cp.start()

    def arrive(cs):
        for cp in cs:
            cp.wait_recv()

    def send_all(src, dst, ssem, rsem):
        to_all(lambda a, o: pltpu.make_async_remote_copy(
            src.at[a * 8 + o], dst.at[me], ssem, rsem, device_id=(a, o), device_id_type=MESH).start())

    def bulk(ref, sem):
        pltpu.make_async_copy(ref.at[pl.ds(0, NDEV - 1)], ref.at[pl.ds(0, NDEV - 1)], sem).wait()

    start(HV)
    start(H[0][0])
    start(H[0][1])

    low = lax.broadcasted_iota(I32, (8, 128), 0) < 4

    def chunk(i, _):
        w_copy(w_hbm, w_ref, wsem, i).wait()
        b = i * 16
        ys = []
        for q in range(8):
            x = sl_ref[pl.ds(pl.multiple_of((b + 2 * q) * 4, 8), 8), :].astype(BF16)
            w = w_ref[pl.ds(b + 2 * q, 2)].reshape(256, 128)
            ys.append(lax.dot_general(x, w, (((1,), (1,)), ((), ())), preferred_element_type=F32))
        for q in range(8):
            cf_ref[pl.ds(pl.multiple_of((b + 2 * q) * 4, 8), 8), :] = jnp.where(low, ys[q][:, 0:128], ys[q][:, 128:256])
        return 0

    packed = pk_ref[...].astype(BF16)
    for q in range(2):
        wide = (widen(ablk_row, q) * 4.0 + field * (1.0 / 32.0))[0:1]
        pick = jnp.where(wide == target[0:64], 1.0, 0.0).astype(BF16)
        sl_ref[pl.ds(512 * q, 512), :] = lax.dot_general(pick, packed, (((0,), (0,)), ((), ())), preferred_element_type=F32)
    lax.fori_loop(0, WCH, chunk, 0)
    place = jnp.where(slot_row[...] == lax.broadcasted_iota(I32, (SLOTS, NBLK), 0), 1.0, 0.0).astype(BF16)
    for f in range(4):
        part = cf_ref[pl.ds(f, NBLK, stride=4), :].astype(BF16)
        sl_ref[pl.ds(f, SLOTS, stride=4), :] = jnp.dot(place, part, preferred_element_type=F32)
    sb_ref[...] = sl_ref[...].astype(BF16).reshape(NDEV, 16, 128)
    send_all(sb_ref, arr, asem.at[0], asem.at[1])
    own = pltpu.make_async_copy(sb_ref.at[me], arr.at[me], asem.at[4])
    own.start()

    def tiles_in(k, g):
        for v in range(3):
            xc[g, v] = merge(hc[k, g, 0, v], hc[k, g, 1, v])

    def coef(l, j):
        return cb[pl.ds(pl.multiple_of((l * 5 + j) * 32, 8), 32), :]

    def advance(l, halo):
        ca, cn, cs, cw, ce = [coef(l, j) for j in range(5)]
        vals = []
        for v in range(3):
            base = (l * 3 + v) * PH
            t = tb[pl.ds(pl.multiple_of(base + 8, 8), 32), :]
            tn = tb[pl.ds(base + 7, 32), :]
            ts = tb[pl.ds(base + 9, 32), :]
            tw, te = sides(t, halo[v], l)
            vals.append(ca * t + cn * tn + cs * ts + cw * tw + ce * te)
        return vals

    def keep(l, vals):
        for v in range(3):
            tb[pl.ds(row_at(l * 3 + v), 32), :] = vals[v]

    def main_round(k, g):
        first, last = GROUPS[g][2:]

        def f(q, _):
            halo = [xc[g, v] for v in range(3)]
            for d in range(4):
                l = 4 * q + 1 + d
                vals = advance(l, halo)
                if k < 3:
                    for v in range(3):
                        put(ec.at[k + 1, g, v], vals[v], l)
                else:
                    vals = [straight(x, l) for x in vals]
                keep(l, vals)
            return 0

        lax.fori_loop(first, last, f, 0)
        if k < 3:
            pack_rows(k + 1, g)
            start(H[k + 1][g])

    def coefs():
        xv = [merge(hcv[0, t], hcv[1, t]) for t in range(2)]
        xc[2, 0] = xv[0]
        xc[2, 1] = xv[1]

        def hrow(i, _):
            for side, row, m in ((0, 7, mn), (1, 40, ms)):
                ub[pl.ds(8 * i * PH + row, 8, stride=PH), :] = hv[side, pl.ds(pl.multiple_of(i * 8, 8), 8), :] * m
            return 0

        lax.fori_loop(0, 10, hrow, 0)

        def one(l):
            base = l * PH
            a = ub[pl.ds(pl.multiple_of(base + 8, 8), 32), :]
            fn = 0.5 * (ub[pl.ds(base + 7, 32), :] + a)
            fs = 0.5 * (a + ub[pl.ds(base + 9, 32), :])
            b = u1[l]
            bw, be = sides(b, xc[2, lax.div(l, 64)], l)
            fw = 0.5 * (bw + b)
            fe = 0.5 * (b + be)
            zero = jnp.zeros_like(a)
            mid = 1.0 - jnp.maximum(fs, zero) + jnp.minimum(fn, zero) - jnp.maximum(fe, zero) + jnp.minimum(fw, zero)
            outs = (mid, jnp.maximum(fn, zero), -jnp.minimum(fs, zero), jnp.maximum(fw, zero), -jnp.minimum(fe, zero))
            return outs

        def f(p, _):
            outs = [one(5 * p + d) for d in range(5)]
            for d in range(5):
                for j in range(5):
                    cb[pl.ds(pl.multiple_of(((5 * p + d) * 5 + j) * 32, 8), 32), :] = outs[d][j]
            return 0

        lax.fori_loop(0, 15, f, 0)

    def step(k, g):
        arrive(H[k][g])
        unpack_rows(k, g)
        tiles_in(k, g)
        main_round(k, g)

    arrive(HV)
    coefs()
    for k in range(2):
        step(k, 0)
        step(k, 1)

    own.wait()
    bulk(arr, asem.at[1])
    summed = jnp.dot(sel[...], arr[...].reshape(2048, 128), preferred_element_type=F32)
    h = jnp.where(kind_ref[...] == 0, 0.0, hx_ref[...])
    den = 1.0 + h * summed[96:128]
    zb = jnp.zeros((32, 128), BF16)
    parts = []
    forced = []
    for v in range(3):
        t0 = tb[pl.ds(v * PH + 8, 32), :]
        surf = jnp.where(kind_ref[...] == 2, ice_ref[v], t0)
        flux = h * (surf - summed[32 * v:32 * v + 32]) / den
        parts.append(flux.astype(BF16))
        t0 = t0 - flux
        tb[pl.ds(v * PH + 8, 32), :] = t0
        forced.append(t0)
    fb = jnp.concatenate(parts + [zb], axis=0)
    ret = lax.dot_general(sel[...], fb, (((0,), (0,)), ((), ())), preferred_element_type=F32)
    rb[...] = ret.astype(BF16).reshape(NDEV, 16, 128)
    send_all(rb, ans_ref, asem.at[2], asem.at[3])
    own2 = pltpu.make_async_copy(rb.at[me], ans_ref.at[me], asem.at[5])
    own2.start()

    def send_zero(k, vals):
        for side, row in ((0, 8), (1, 39)):
            er0[k, side, :, :] = tb[pl.ds(row, 8, stride=PH), :]
        for v in range(3):
            ec0[k, v] = vals[v]
        start(H0[k])

    def recv_zero(k):
        arrive(H0[k])
        for side, row, m in ((0, 7, mn), (1, 40, ms)):
            tb[pl.ds(row, 3, stride=PH), :] = hr0[k, side, 0:3, :] * m
        vals = advance(0, [merge(hc0[k, 0, v], hc0[k, 1, v]) for v in range(3)])
        keep(0, vals)
        return vals

    def put_out(l0, l1, j):
        cs = [pltpu.make_async_copy(tb4.at[pl.ds(l0, l1 - l0), v, pl.ds(8, 32)], oc_hbm.at[v, pl.ds(l0, l1 - l0)], osem.at[j + v]) for v in range(3)]
        start(cs)
        return cs

    send_zero(0, forced)
    step(2, 0)
    send_zero(1, recv_zero(0))
    step(2, 1)
    send_zero(2, recv_zero(1))
    step(3, 0)
    outs = put_out(1, 41, 0)
    send_zero(3, recv_zero(2))
    step(3, 1)
    outs = outs + put_out(41, OL, 3)
    recv_zero(3)
    outs = outs + put_out(0, 1, 6)
    own2.wait()
    for cp in cg:
        cp.wait()
    bulk(ans_ref, asem.at[3])
    bulk(sb_ref, asem.at[0])
    bulk(rb, asem.at[2])
    for cs in [c for pair in H for c in pair] + [HV] + H0:
        for cp in cs:
            cp.wait_send()
    for cp in outs:
        cp.wait()


def rk(slot, ablk, recv, atm, dif, w, tracer, velocity, hx, kind, ice):
    D = pltpu.SemaphoreType.DMA
    V = pltpu.VMEM
    S = jax.ShapeDtypeStruct
    return pl.pallas_call(
        rk_body,
        out_shape=(S((NDEV, 16, 128), BF16), S((3, OL, 32, 128), F32),
                   S((1024, 128), F32), S((NV, 1024, 128), F32), S((16, 128), F32)),
        in_specs=[VM, VM, VM, ANY, ANY, ANY, ANY, ANY, ANY, ANY, ANY],
        out_specs=(VM, ANY, ANY, ANY, VM),
        scratch_shapes=[
            V((NBLK, 128, 128), BF16), V((NV, LEV, 2048), F32), V((LEV - 1, 2048), F32), V((1024, 128), F32), V((NV, 1024, 128), F32),
            V((NV * 1024, 128), F32), V((1024, 128), F32), V((64, 128), F32), V((1024, 128), F32), V((2048, 128), F32),
            V((NDEV, 16, 128), BF16), D((WCH,)), D((4,)),
            V((32, 128), F32), V((32, 128), I32), V((3, 32, 128), F32), V((PLANES * PH, 128), F32), V((77 * 5 * 32, 128), F32), V((80 * PH, 128), F32), V((OL, 32, 128), F32),
            V((4, 2, 2, 120, 128), F32), V((4, 2, 2, 120, 128), F32), V((4, 2, 3, 32, 128), F32), V((4, 2, 2, 3, 32, 128), F32),
            V((2, 80, 128), F32), V((2, 80, 128), F32), V((2, 32, 128), F32), V((2, 2, 32, 128), F32), V((3, 3, 32, 128), F32),
            V((4, 2, 8, 128), F32), V((4, 2, 8, 128), F32), V((4, 3, 32, 128), F32), V((4, 2, 3, 32, 128), F32),
            V((NDEV, 16, 128), BF16), V((NDEV, 16, 128), BF16), V((128, 2048), BF16),
            D((8,)), D((9,)), D((4, 2, 4)), D((4, 2, 4)), D((4,)), D((4,)), D((4, 4)), D((4, 4)), D((6,)),
        ],
        compiler_params=pltpu.CompilerParams(collective_id=0, has_side_effects=True, vmem_limit_bytes=62 << 20),
        name="exchange_ocean",
    )(ablk, slot, recv, atm, dif, w, tracer, velocity, hx, kind, ice)

def per_device(atm_state, diffusivity, send_slot, atm_block, recv_row, remap_weight, ocean_tracer, ocean_velocity,
               exchange_coef, surface_kind, ice_surface):
    ans, ocean, c, g, r = rk(send_slot, atm_block, recv_row, atm_state, diffusivity, remap_weight, ocean_tracer, ocean_velocity,
                             exchange_coef, surface_kind, ice_surface)
    return k3(send_slot, atm_block, ans.reshape(2048, 128), remap_weight, c, g, r, ocean)


def solution(mesh):
    placed = (
        P(None, None, ("atm", "ocn")),
        P(None, ("atm", "ocn")),
        P(("atm", "ocn"), None),
        P(("atm", "ocn"), None),
        P(("atm", "ocn"), None),
        P(("atm", "ocn"), None, None),
        P(None, None, "atm", "ocn"),
        P(None, None, "atm", "ocn"),
        P("atm", "ocn"),
        P("atm", "ocn"),
        P(None, "atm", "ocn"),
    )
    return jax.shard_map(
        per_device,
        mesh=mesh,
        in_specs=placed,
        out_specs=(P(None, None, ("atm", "ocn")), P(None, None, "atm", "ocn")),
        check_vma=False,
    )
```

```python
import functools
import jax
import jax.numpy as jnp
from jax import lax
from jax.experimental import pallas as pl
from jax.experimental.pallas import tpu as pltpu
from jax.sharding import PartitionSpec as P

F32, BF16, I32 = jnp.float32, jnp.bfloat16, jnp.int32
MESH = pl.DeviceIdType.MESH
VM = pl.BlockSpec(memory_space=pltpu.VMEM)
SM = pl.BlockSpec(memory_space=pltpu.SMEM)
ANY = pl.BlockSpec(memory_space=pltpu.HBM)
NV, LEV, NBLK, AB, SLOTS = 3, 63, 256, 16, 512
WCH = 16


def w_copy(w_hbm, w_ref, sem, i):
    n = NBLK // WCH
    rows = pl.ds(i * n, n)
    return pltpu.make_async_copy(w_hbm.at[rows], w_ref.at[rows], sem.at[i])


def w_copies(w_hbm, w_ref, sem):
    return [w_copy(w_hbm, w_ref, sem, i) for i in range(WCH)]


def k3_body(slot_ref, ablk_ref, ans_ref, w_hbm, c_hbm, g_hbm, r_ref, oc_in, out_hbm, oc_out,
            w_ref, c_ref, g_ref, oc_ref, af_ref, acc_ref, x_ref, out_ref, sem, isem, osem):
    cps = w_copies(w_hbm, w_ref, sem)
    ins = [pltpu.make_async_copy(c_hbm, c_ref, isem.at[0]), pltpu.make_async_copy(g_hbm, g_ref, isem.at[1])]
    oin = pltpu.make_async_copy(oc_in, oc_ref, isem.at[2])
    oout = pltpu.make_async_copy(oc_ref, oc_out, isem.at[3])
    for cp in cps + ins:
        cp.start()
    oin.start()
    af_ref[...] = ans_ref[...].astype(F32)
    acc_ref[...] = jnp.zeros_like(acc_ref)
    zero = jnp.zeros((4, 128), F32)

    def chunk(i, _):
        w_copy(w_hbm, w_ref, sem, i).wait()
        b = i * 16
        ys = []
        for q in range(8):
            x0 = af_ref[pl.ds(pl.multiple_of(slot_ref[0, b + 2 * q] * 4, 4), 4), :]
            x1 = af_ref[pl.ds(pl.multiple_of(slot_ref[0, b + 2 * q + 1] * 4, 4), 4), :]
            top = jnp.concatenate([x0, zero], axis=0)
            bot = jnp.concatenate([zero, x1], axis=0)
            x = jnp.concatenate([top, bot], axis=1).astype(BF16)
            ys.append(jnp.dot(x, w_ref[pl.ds(b + 2 * q, 2)].reshape(256, 128), preferred_element_type=F32))
        for j in range(16):
            m = pl.multiple_of(ablk_ref[0, b + j] * 8, 8)
            e = j % 2
            acc_ref[j % 8, pl.ds(m, 4), :] = acc_ref[j % 8, pl.ds(m, 4), :] + ys[j // 2][4 * e:4 * e + 4]
        return 0

    lax.fori_loop(0, WCH, chunk, 0)
    tot = acc_ref[0]
    for j in range(1, 8):
        tot = tot + acc_ref[j]
    acc_ref[0] = tot
    for cp in ins:
        cp.wait()
    oin.wait()
    oout.start()
    r = r_ref[...]
    xs = []
    for v in range(NV):
        sf = acc_ref[0, pl.ds(v, 16, stride=8), :]
        x = g_ref[v, pl.ds((LEV - 1) * 16, 16), :] + r * sf
        x_ref[pl.ds(v * 1024 + (LEV - 1) * 16, 16), :] = x
        xs.append(x)

    def down(k, xs):
        c = c_ref[pl.ds(k * 16, 16), :]
        new = []
        for v in range(NV):
            x = g_ref[v, pl.ds(k * 16, 16), :] - c * xs[v]
            x_ref[pl.ds(v * 1024 + k * 16, 16), :] = x
            new.append(x)
        return new

    def rows_out(i, n):
        for v in range(NV):
            for j in range(16):
                out_ref[v, pl.ds(8 * i, n), pl.ds(128 * j, 128)] = x_ref[pl.ds(v * 1024 + 8 * i * 16 + j, n, stride=16), :]

    for k in range(LEV - 2, 55, -1):
        xs = down(k, xs)
    rows_out(7, 7)

    def group(q, xs):
        i = 6 - q
        for d in range(8):
            xs = down(8 * i + 7 - d, xs)
        rows_out(i, 8)
        return xs

    lax.fori_loop(0, 7, group, xs)
    res = pltpu.make_async_copy(out_ref, out_hbm, osem)
    res.start()
    oout.wait()
    res.wait()


def k3(slot, ablk, ans, w, c, g, r, ocean):
    V = pltpu.VMEM
    return pl.pallas_call(
        k3_body,
        out_shape=(jax.ShapeDtypeStruct((NV, LEV, 2048), F32), jax.ShapeDtypeStruct((3, 75, 32, 128), F32)),
        in_specs=[SM, SM, VM, ANY, ANY, ANY, VM, ANY],
        out_specs=(ANY, ANY),
        scratch_shapes=[V((NBLK, 128, 128), BF16), V((1024, 128), F32), V((NV, 1024, 128), F32), V((3, 75, 32, 128), F32),
                        V((2048, 128), F32), V((8, 128, 128), F32), V((NV * 1024, 128), F32), V((NV, LEV, 2048), F32),
                        pltpu.SemaphoreType.DMA((WCH,)), pltpu.SemaphoreType.DMA((4,)), pltpu.SemaphoreType.DMA],
        compiler_params=pltpu.CompilerParams(vmem_limit_bytes=62 << 20), name="backward_up",
    )(slot, ablk, ans, w, c, g, r, ocean)

NDEV, OL, PH = 128, 75, 48
PLANES = 231
GROUPS = ((3, 15, 0, 10), (123, 13, 10, 19))


def rk_body(ablk_row, slot_row, val_ref, atm_hbm, dif_hbm, w_hbm, tr_hbm, ve_hbm, hx_hbm, kind_hbm, ice_hbm,
            ans_ref, oc_hbm, c_hbm, g_hbm, r_ref,
            w_ref, atm_ref, dif_ref, c_ref, g_ref, s_ref, d_ref, pk_ref, cf_ref, sl_ref, sb_ref, wsem, isem,
            hx_ref, kind_ref, ice_ref, tb, cb, ub, u1, er, hr, ec, hc, ev, hv, cv, hcv, xc, er0, hr0, ec0, hc0, arr, rb, sel,
            lsem, osem, hs, hrs, hsv, hrv, hs0, hr0s, asem):
    A = lax.axis_index("atm")
    O = lax.axis_index("ocn")
    me = A * 8 + O

    ins = [pltpu.make_async_copy(atm_hbm, atm_ref, isem.at[0]), pltpu.make_async_copy(dif_hbm, dif_ref, isem.at[1])]
    for cp in ins:
        cp.start()
    loads = []
    tb4 = tb.reshape(PLANES // 3, 3, PH, 128)
    ub3 = ub.reshape(80, PH, 128)
    for v in range(3):
        loads.append(pltpu.make_async_copy(tr_hbm.at[v], tb4.at[pl.ds(0, OL), v, pl.ds(8, 32)], lsem.at[v]))
    loads.append(pltpu.make_async_copy(ve_hbm.at[0], ub3.at[pl.ds(0, OL), pl.ds(8, 32)], lsem.at[3]))
    loads.append(pltpu.make_async_copy(ve_hbm.at[1], u1, lsem.at[4]))
    for i, (a, b) in enumerate(((hx_hbm, hx_ref), (kind_hbm, kind_ref), (ice_hbm, ice_ref))):
        loads.append(pltpu.make_async_copy(a, b, lsem.at[5 + i]))
    loads = loads[3:5] + loads[:3] + loads[5:]
    for cp in loads + w_copies(w_hbm, w_ref, wsem):
        cp.start()

    bar = pltpu.get_barrier_semaphore()

    cols = [lax.rem(O + j, 8) for j in range(8)]

    def to_all(fn):
        for j in range(1, 8):
            fn(A, cols[j])

        def f(i, _):
            a = lax.rem(A + i, 16)
            for j in range(8):
                fn(a, cols[j])
            return 0

        lax.fori_loop(1, 16, f, 0)

    to_all(lambda a, o: pl.semaphore_signal(bar, inc=1, device_id=(a, o), device_id_type=MESH))

    lane = lax.broadcasted_iota(I32, (32, 128), 1)
    mn = jnp.where(A > 0, 1.0, 0.0).astype(F32)
    ms = jnp.where(A < 15, 1.0, 0.0).astype(F32)
    mw = jnp.where(O > 0, 1.0, 0.0).astype(F32)
    mx = jnp.where(O < 7, 1.0, 0.0).astype(F32)

    for cp in ins:
        cp.wait()
    for v in range(NV + 1):
        rows = LEV if v < NV else LEV - 1
        for i in range(8):
            n = min(8, rows - 8 * i)
            for j in range(16):
                src = atm_ref[v, pl.ds(8 * i, n), pl.ds(128 * j, 128)] if v < NV else dif_ref[pl.ds(8 * i, n), pl.ds(128 * j, 128)]
                if v < NV:
                    s_ref[pl.ds(v * 1024 + 8 * i * 16 + j, n, stride=16), :] = src
                else:
                    d_ref[pl.ds(8 * i * 16 + j, n, stride=16), :] = src

    def level(k, kprev, know, c, g):
        den = 1.0 + kprev + know + kprev * c
        r = 1.0 / den
        gn = []
        for v in range(NV):
            gv = (s_ref[pl.ds(v * 1024 + k * 16, 16), :] + kprev * g[v]) * r
            g_ref[v, pl.ds(k * 16, 16), :] = gv
            gn.append(gv)
        return r, gn

    z = jnp.zeros((16, 128), F32)

    def step(k, carry):
        kprev, c, g = carry
        know = d_ref[pl.ds(k * 16, 16), :]
        r, gn = level(k, kprev, know, c, g)
        cn = -know * r
        c_ref[pl.ds(k * 16, 16), :] = cn
        return know, cn, gn

    kprev, c, g = lax.fori_loop(0, LEV - 1, step, (z, z, [z, z, z]), unroll=2)
    r, g = level(LEV - 1, kprev, z, c, g)
    r_ref[...] = r
    for f in range(4):
        val = g[f] if f < 3 else r
        pk_ref[pl.ds(f, 16, stride=4), :] = val
    cg = [pltpu.make_async_copy(c_ref, c_hbm, isem.at[2]), pltpu.make_async_copy(g_ref, g_hbm, isem.at[3])]
    for cp in cg:
        cp.start()

    spread = jnp.where(lax.broadcasted_iota(I32, (128, 512), 1) // 4 == lax.broadcasted_iota(I32, (128, 512), 0), 1.0, 0.0).astype(BF16)
    field = lax.rem(lax.broadcasted_iota(I32, (8, 512), 1), 4).astype(F32) * 32.0
    target = lax.broadcasted_iota(I32, (128, 512), 0).astype(F32)


    def widen(ref, q):
        rows = jnp.broadcast_to(ref[:, pl.ds(128 * q, 128)].astype(F32), (8, 128)).astype(BF16)
        return jnp.dot(rows, spread, preferred_element_type=F32)

    tb[pl.ds(OL * 3 * PH, 6 * PH), :] = jnp.zeros((6 * PH, 128), F32)
    ub[pl.ds(OL * PH, 5 * PH), :] = jnp.zeros((5 * PH, 128), F32)
    ec[...] = jnp.zeros_like(ec)
    cv[...] = jnp.zeros_like(cv)
    for cp in loads:
        cp.wait()

    def pack_rows(k, g):
        p0, n = GROUPS[g][:2]

        def f(i, _):
            for side, row in ((0, 8), (1, 39)):
                er[k, g, side, pl.ds(pl.multiple_of(i * 8, 8), 8), :] = tb[pl.ds((p0 + 8 * i) * PH + row, 8, stride=PH), :]
            return 0
        lax.fori_loop(0, n, f, 0)

    def unpack_rows(k, g):
        p0, n = GROUPS[g][:2]

        def f(i, _):
            for side, row, m in ((0, 7, mn), (1, 40, ms)):
                tb[pl.ds((p0 + 8 * i) * PH + row, 8, stride=PH), :] = hr[k, g, side, pl.ds(pl.multiple_of(i * 8, 8), 8), :] * m
            return 0
        lax.fori_loop(0, n, f, 0)

    couple = lax.rem(lane + 1, 128) // 2
    even = lax.rem(lane, 2) == 0

    def turn_of(l):
        return lax.rem(l, 64)

    def turned(x, l):
        return pltpu.roll(x, 2 * turn_of(l), 1)

    def straight(x, l):
        return pltpu.roll(x, lax.rem(128 - 2 * turn_of(l), 128), 1)

    def put(ref_view, val, l):
        pltpu.store(ref_view, val, mask=couple == turn_of(l))

    def merge(w, e):
        return jnp.where(even, pltpu.roll(w, 1, 1) * mw, pltpu.roll(e, 127, 1) * mx)

    def sides(x, h, l):
        here = couple == turn_of(l)
        tw = jnp.where(here & even, h, pltpu.roll(x, 1, 1))
        te = jnp.where(here & ~even, h, pltpu.roll(x, 127, 1))
        return tw, te

    def row_at(p):
        return pl.multiple_of(p * PH + 8, 8)

    def first_turn(g):
        def f(q, _):
            for d in range(4):
                l = 4 * q + 1 + d
                for v in range(3):
                    x = turned(tb[pl.ds(row_at(l * 3 + v), 32), :], l)
                    tb[pl.ds(row_at(l * 3 + v), 32), :] = x
                    put(ec.at[0, g, v], x, l)
            return 0
        lax.fori_loop(GROUPS[g][2], GROUPS[g][3], f, 0)
        pack_rows(0, g)

    def vturn(p, _):
        for d in range(5):
            l = 5 * p + d
            x = turned(u1[l], l)
            u1[l] = x
            put(cv.at[lax.div(l, 64)], x, l)
            row = pl.ds(pl.multiple_of(l * PH + 8, 8), 32)
            ub[row, :] = turned(ub[row, :], l)
        return 0

    lax.fori_loop(0, 15, vturn, 0)

    def uedge(i, _):
        for side, row in ((0, 8), (1, 39)):
            ev[side, pl.ds(pl.multiple_of(i * 8, 8), 8), :] = ub[pl.ds(8 * i * PH + row, 8, stride=PH), :]
        return 0

    lax.fori_loop(0, 10, uedge, 0)
    first_turn(0)
    first_turn(1)

    up = (lax.rem(A + 15, 16), O)
    down = (lax.rem(A + 1, 16), O)
    west = (A, lax.rem(O + 7, 8))
    east = (A, lax.rem(O + 1, 8))
    mk = pltpu.make_async_remote_copy

    def halo(k, g):
        rows = pl.ds(0, 8 * GROUPS[g][1])
        return [
            mk(er.at[k, g, 0, rows], hr.at[k, g, 1, rows], hs.at[k, g, 0], hrs.at[k, g, 0], device_id=up, device_id_type=MESH),
            mk(er.at[k, g, 1, rows], hr.at[k, g, 0, rows], hs.at[k, g, 1], hrs.at[k, g, 1], device_id=down, device_id_type=MESH),
            mk(ec.at[k, g], hc.at[k, g, 1], hs.at[k, g, 2], hrs.at[k, g, 2], device_id=west, device_id_type=MESH),
            mk(ec.at[k, g], hc.at[k, g, 0], hs.at[k, g, 3], hrs.at[k, g, 3], device_id=east, device_id_type=MESH),
        ]

    def halo0(k):
        return [
            mk(er0.at[k, 0], hr0.at[k, 1], hs0.at[k, 0], hr0s.at[k, 0], device_id=up, device_id_type=MESH),
            mk(er0.at[k, 1], hr0.at[k, 0], hs0.at[k, 1], hr0s.at[k, 1], device_id=down, device_id_type=MESH),
            mk(ec0.at[k], hc0.at[k, 1], hs0.at[k, 2], hr0s.at[k, 2], device_id=west, device_id_type=MESH),
            mk(ec0.at[k], hc0.at[k, 0], hs0.at[k, 3], hr0s.at[k, 3], device_id=east, device_id_type=MESH),
        ]

    pl.semaphore_wait(bar, NDEV - 1)
    H = [[halo(k, g) for g in range(2)] for k in range(4)]
    HV = [
        mk(ev.at[0], hv.at[1], hsv.at[0], hrv.at[0], device_id=up, device_id_type=MESH),
        mk(ev.at[1], hv.at[0], hsv.at[1], hrv.at[1], device_id=down, device_id_type=MESH),
        mk(cv, hcv.at[1], hsv.at[2], hrv.at[2], device_id=west, device_id_type=MESH),
        mk(cv, hcv.at[0], hsv.at[3], hrv.at[3], device_id=east, device_id_type=MESH),
    ]
    H0 = [halo0(k) for k in range(4)]

    def start(cs):
        for cp in cs:
            cp.start()

    def arrive(cs):
        for cp in cs:
            cp.wait_recv()

    def send_all(src, dst, ssem, rsem):
        to_all(lambda a, o: pltpu.make_async_remote_copy(
            src.at[a * 8 + o], dst.at[me], ssem, rsem, device_id=(a, o), device_id_type=MESH).start())

    def bulk(ref, sem):
        pltpu.make_async_copy(ref.at[pl.ds(0, NDEV - 1)], ref.at[pl.ds(0, NDEV - 1)], sem).wait()

    start(HV)
    start(H[0][0])
    start(H[0][1])

    low = lax.broadcasted_iota(I32, (8, 128), 0) < 4

    def chunk(i, _):
        w_copy(w_hbm, w_ref, wsem, i).wait()
        b = i * 16
        ys = []
        for q in range(8):
            x = sl_ref[pl.ds(pl.multiple_of((b + 2 * q) * 4, 8), 8), :].astype(BF16)
            w = w_ref[pl.ds(b + 2 * q, 2)].reshape(256, 128)
            ys.append(lax.dot_general(x, w, (((1,), (1,)), ((), ())), preferred_element_type=F32))
        for q in range(8):
            cf_ref[pl.ds(pl.multiple_of((b + 2 * q) * 4, 8), 8), :] = jnp.where(low, ys[q][:, 0:128], ys[q][:, 128:256])
        return 0

    packed = pk_ref[...].astype(BF16)
    for q in range(2):
        wide = (widen(ablk_row, q) * 4.0 + field * (1.0 / 32.0))[0:1]
        pick = jnp.where(wide == target[0:64], 1.0, 0.0).astype(BF16)
        sl_ref[pl.ds(512 * q, 512), :] = lax.dot_general(pick, packed, (((0,), (0,)), ((), ())), preferred_element_type=F32)
    lax.fori_loop(0, WCH, chunk, 0)
    place = jnp.where(slot_row[...] == lax.broadcasted_iota(I32, (SLOTS, NBLK), 0), 1.0, 0.0).astype(BF16)
    for f in range(4):
        part = cf_ref[pl.ds(f, NBLK, stride=4), :].astype(BF16)
        sl_ref[pl.ds(f, SLOTS, stride=4), :] = jnp.dot(place, part, preferred_element_type=F32)
    sb_ref[...] = sl_ref[...].astype(BF16).reshape(NDEV, 16, 128)
    send_all(sb_ref, arr, asem.at[0], asem.at[1])
    cb[pl.ds(OL * 5 * 32, 2 * 5 * 32), :] = jnp.zeros((2 * 5 * 32, 128), F32)
    ec0[...] = jnp.zeros_like(ec0)
    for q in range(4):
        wide = widen(val_ref, q)
        wide = jnp.where(wide >= 0.0, wide + field, -1.0)[0:1]
        sel[:, pl.ds(512 * q, 512)] = jnp.where(wide == target, 1.0, 0.0).astype(BF16)
    own = pltpu.make_async_copy(sb_ref.at[me], arr.at[me], asem.at[4])
    own.start()

    def tiles_in(k, g):
        for v in range(3):
            xc[g, v] = merge(hc[k, g, 0, v], hc[k, g, 1, v])

    def coef(l, j):
        return cb[pl.ds(pl.multiple_of((l * 5 + j) * 32, 8), 32), :]

    def advance(l, halo):
        ca, cn, cs, cw, ce = [coef(l, j) for j in range(5)]
        vals = []
        for v in range(3):
            base = (l * 3 + v) * PH
            t = tb[pl.ds(pl.multiple_of(base + 8, 8), 32), :]
            tn = tb[pl.ds(base + 7, 32), :]
            ts = tb[pl.ds(base + 9, 32), :]
            tw, te = sides(t, halo[v], l)
            vals.append(ca * t + cn * tn + cs * ts + cw * tw + ce * te)
        return vals

    def keep(l, vals):
        for v in range(3):
            tb[pl.ds(row_at(l * 3 + v), 32), :] = vals[v]

    def main_round(k, g):
        first, last = GROUPS[g][2:]

        def f(q, _):
            halo = [xc[g, v] for v in range(3)]
            for d in range(4):
                l = 4 * q + 1 + d
                vals = advance(l, halo)
                if k < 3:
                    for v in range(3):
                        put(ec.at[k + 1, g, v], vals[v], l)
                else:
                    vals = [straight(x, l) for x in vals]
                keep(l, vals)
            return 0

        lax.fori_loop(first, last, f, 0)
        if k < 3:
            pack_rows(k + 1, g)
            start(H[k + 1][g])

    def coefs():
        xv = [merge(hcv[0, t], hcv[1, t]) for t in range(2)]
        xc[2, 0] = xv[0]
        xc[2, 1] = xv[1]

        def hrow(i, _):
            for side, row, m in ((0, 7, mn), (1, 40, ms)):
                ub[pl.ds(8 * i * PH + row, 8, stride=PH), :] = hv[side, pl.ds(pl.multiple_of(i * 8, 8), 8), :] * m
            return 0

        lax.fori_loop(0, 10, hrow, 0)

        def one(l):
            base = l * PH
            a = ub[pl.ds(pl.multiple_of(base + 8, 8), 32), :]
            fn = 0.5 * (ub[pl.ds(base + 7, 32), :] + a)
            fs = 0.5 * (a + ub[pl.ds(base + 9, 32), :])
            b = u1[l]
            bw, be = sides(b, xc[2, lax.div(l, 64)], l)
            fw = 0.5 * (bw + b)
            fe = 0.5 * (b + be)
            zero = jnp.zeros_like(a)
            mid = 1.0 - jnp.maximum(fs, zero) + jnp.minimum(fn, zero) - jnp.maximum(fe, zero) + jnp.minimum(fw, zero)
            outs = (mid, jnp.maximum(fn, zero), -jnp.minimum(fs, zero), jnp.maximum(fw, zero), -jnp.minimum(fe, zero))
            return outs

        def f(p, _):
            outs = [one(5 * p + d) for d in range(5)]
            for d in range(5):
                for j in range(5):
                    cb[pl.ds(pl.multiple_of(((5 * p + d) * 5 + j) * 32, 8), 32), :] = outs[d][j]
            return 0

        lax.fori_loop(0, 15, f, 0)

    def step(k, g):
        arrive(H[k][g])
        unpack_rows(k, g)
        tiles_in(k, g)
        main_round(k, g)

    arrive(HV)
    coefs()
    for k in range(2):
        step(k, 0)
        step(k, 1)

    own.wait()
    bulk(arr, asem.at[1])
    summed = jnp.dot(sel[...], arr[...].reshape(2048, 128), preferred_element_type=F32)
    h = jnp.where(kind_ref[...] == 0, 0.0, hx_ref[...])
    den = 1.0 + h * summed[96:128]
    zb = jnp.zeros((32, 128), BF16)
    parts = []
    forced = []
    for v in range(3):
        t0 = tb[pl.ds(v * PH + 8, 32), :]
        surf = jnp.where(kind_ref[...] == 2, ice_ref[v], t0)
        flux = h * (surf - summed[32 * v:32 * v + 32]) / den
        parts.append(flux.astype(BF16))
        t0 = t0 - flux
        tb[pl.ds(v * PH + 8, 32), :] = t0
        forced.append(t0)
    fb = jnp.concatenate(parts + [zb], axis=0)
    ret = lax.dot_general(sel[...], fb, (((0,), (0,)), ((), ())), preferred_element_type=F32)
    rb[...] = ret.astype(BF16).reshape(NDEV, 16, 128)
    send_all(rb, ans_ref, asem.at[2], asem.at[3])
    own2 = pltpu.make_async_copy(rb.at[me], ans_ref.at[me], asem.at[5])
    own2.start()

    def send_zero(k, vals):
        for side, row in ((0, 8), (1, 39)):
            er0[k, side, :, :] = tb[pl.ds(row, 8, stride=PH), :]
        for v in range(3):
            ec0[k, v] = vals[v]
        start(H0[k])

    def recv_zero(k):
        arrive(H0[k])
        for side, row, m in ((0, 7, mn), (1, 40, ms)):
            tb[pl.ds(row, 3, stride=PH), :] = hr0[k, side, 0:3, :] * m
        vals = advance(0, [merge(hc0[k, 0, v], hc0[k, 1, v]) for v in range(3)])
        keep(0, vals)
        return vals

    def put_out(l0, l1, j):
        cs = [pltpu.make_async_copy(tb4.at[pl.ds(l0, l1 - l0), v, pl.ds(8, 32)], oc_hbm.at[v, pl.ds(l0, l1 - l0)], osem.at[j + v]) for v in range(3)]
        start(cs)
        return cs

    send_zero(0, forced)
    step(2, 0)
    send_zero(1, recv_zero(0))
    step(2, 1)
    send_zero(2, recv_zero(1))
    step(3, 0)
    outs = put_out(1, 41, 0)
    send_zero(3, recv_zero(2))
    step(3, 1)
    outs = outs + put_out(41, OL, 3)
    recv_zero(3)
    outs = outs + put_out(0, 1, 6)
    own2.wait()
    for cp in cg:
        cp.wait()
    bulk(ans_ref, asem.at[3])
    bulk(sb_ref, asem.at[0])
    bulk(rb, asem.at[2])
    for cs in [c for pair in H for c in pair] + [HV] + H0:
        for cp in cs:
            cp.wait_send()
    for cp in outs:
        cp.wait()


def rk(slot, ablk, recv, atm, dif, w, tracer, velocity, hx, kind, ice):
    D = pltpu.SemaphoreType.DMA
    V = pltpu.VMEM
    S = jax.ShapeDtypeStruct
    return pl.pallas_call(
        rk_body,
        out_shape=(S((NDEV, 16, 128), BF16), S((3, OL, 32, 128), F32),
                   S((1024, 128), F32), S((NV, 1024, 128), F32), S((16, 128), F32)),
        in_specs=[VM, VM, VM, ANY, ANY, ANY, ANY, ANY, ANY, ANY, ANY],
        out_specs=(VM, ANY, ANY, ANY, VM),
        scratch_shapes=[
            V((NBLK, 128, 128), BF16), V((NV, LEV, 2048), F32), V((LEV - 1, 2048), F32), V((1024, 128), F32), V((NV, 1024, 128), F32),
            V((NV * 1024, 128), F32), V((1024, 128), F32), V((64, 128), F32), V((1024, 128), F32), V((2048, 128), F32),
            V((NDEV, 16, 128), BF16), D((WCH,)), D((4,)),
            V((32, 128), F32), V((32, 128), I32), V((3, 32, 128), F32), V((PLANES * PH, 128), F32), V((77 * 5 * 32, 128), F32), V((80 * PH, 128), F32), V((OL, 32, 128), F32),
            V((4, 2, 2, 120, 128), F32), V((4, 2, 2, 120, 128), F32), V((4, 2, 3, 32, 128), F32), V((4, 2, 2, 3, 32, 128), F32),
            V((2, 80, 128), F32), V((2, 80, 128), F32), V((2, 32, 128), F32), V((2, 2, 32, 128), F32), V((3, 3, 32, 128), F32),
            V((4, 2, 8, 128), F32), V((4, 2, 8, 128), F32), V((4, 3, 32, 128), F32), V((4, 2, 3, 32, 128), F32),
            V((NDEV, 16, 128), BF16), V((NDEV, 16, 128), BF16), V((128, 2048), BF16),
            D((8,)), D((9,)), D((4, 2, 4)), D((4, 2, 4)), D((4,)), D((4,)), D((4, 4)), D((4, 4)), D((6,)),
        ],
        compiler_params=pltpu.CompilerParams(collective_id=0, has_side_effects=True, vmem_limit_bytes=62 << 20),
        name="exchange_ocean",
    )(ablk, slot, recv, atm, dif, w, tracer, velocity, hx, kind, ice)

def per_device(atm_state, diffusivity, send_slot, atm_block, recv_row, remap_weight, ocean_tracer, ocean_velocity,
               exchange_coef, surface_kind, ice_surface):
    ans, ocean, c, g, r = rk(send_slot, atm_block, recv_row, atm_state, diffusivity, remap_weight, ocean_tracer, ocean_velocity,
                             exchange_coef, surface_kind, ice_surface)
    return k3(send_slot, atm_block, ans.reshape(2048, 128), remap_weight, c, g, r, ocean)


def solution(mesh):
    placed = (
        P(None, None, ("atm", "ocn")),
        P(None, ("atm", "ocn")),
        P(("atm", "ocn"), None),
        P(("atm", "ocn"), None),
        P(("atm", "ocn"), None),
        P(("atm", "ocn"), None, None),
        P(None, None, "atm", "ocn"),
        P(None, None, "atm", "ocn"),
        P("atm", "ocn"),
        P("atm", "ocn"),
        P(None, "atm", "ocn"),
    )
    return jax.shard_map(
        per_device,
        mesh=mesh,
        in_specs=placed,
        out_specs=(P(None, None, ("atm", "ocn")), P(None, None, "atm", "ocn")),
        check_vma=False,
    )
```
